256 devices in a mesh: grid: 16 (over y, x), mic: 4 (over z_hi), bin: 4 (over z_lo, core).
Axes of the slice: x: 4, y: 4, z: 8 (z_hi: 4, z_lo: 2; z = z_hi * 2 + z_lo), core: 2. Of those that a mesh axis runs over, the one named last changes fastest.
Arguments:
- grid_points: float32 [3, 16384], P(None, 'grid'), may hold values from -1 to 3, as said below
- mic_coords: float32 [3, 4096], P(None, 'mic'), may hold values from -1 to 1, as said below
- wavenumbers: float32 [16], P('bin'), may hold values from 20 to 150
- pressures: float32 [16, 2, 16, 4096], P('bin', None, None, 'mic'), may hold values from -6 to 6
Outputs:
- solution: float32 [16, 2, 16, 16384], P('bin', None, None, 'grid')
- residual: float32 [16, 2, 16, 4096], P('bin', None, None, 'mic')
The draws below stay inside these ranges and needn't reach their ends.
Inputs may be any that keep to these rules, and one draw needn't show every extreme that they name: `grid_points`: rows 0 and 1 lie in -1 to 1, row 2 in 1 to 3. `mic_coords`: rows 0 and 1 lie in -1 to 1, row 2 in -0.05 to 0.05.
All inputs are finite; a program needn't handle non-finite values.
Results may differ from the reference program's by a relative error of at most 0.0055.
Values may be sent and summed in bfloat16 or wider, within the bound.
No kernel may reach another device: no remote copies, remote signals or barrier semaphores. Data moves between devices by JAX's collectives and lax.ppermute only.
A program may use at most 64 MiB of HBM per device.

```python
import math
import jax
import jax.numpy as jnp
from jax import lax

BINS = 16
SNAPS = 16
MICS = 4096
GRID_DEV = 1024
ITERS = 2
GRID = 16384


def draw_grid_points(key, part):
    base = jax.random.uniform(key, (3, GRID), jnp.float32, -1.0, 1.0)
    lift = jnp.array([0.0, 0.0, 2.0], jnp.float32)[:, None]
    return base + lift


def draw_mic_coords(key, part):
    base = jax.random.uniform(key, (3, MICS), jnp.float32, -1.0, 1.0)
    squash = jnp.array([1.0, 1.0, 0.05], jnp.float32)[:, None]
    return base * squash


def shard_levels(rng, dims, pieces, smallest, high):
    def one(position, parts):
        heights = jax.random.uniform(jax.random.fold_in(jax.random.fold_in(rng, 6), position), (parts,), jnp.float32, smallest / len(pieces), high / len(pieces))
        return jnp.repeat(jnp.exp(heights), dims[position] // parts).reshape((-1,) + (1,) * (len(dims) - position - 1))

    factor_of = one(*pieces[0])
    for cut in pieces[1:]:
        factor_of = factor_of * one(*cut)
    return factor_of


def normal_values(stream_key, extent, spread, bound, cuts=(), held_as=jnp.bfloat16):
    drawn = jax.random.normal(stream_key, extent, jnp.float32) * spread
    if len(cuts) > 0:
        drawn = shard_levels(stream_key, extent, cuts, -0.22, 0.18) * drawn
    return jnp.clip(drawn, min=-bound, max=bound).astype(held_as)


def setup_inputs(seed: int = 0) -> dict:
    seeds = jax.random.split(jax.random.key(seed), 5)
    grid_points = draw_grid_points(jax.random.fold_in(seeds[4], 71), 0)
    mic_coords = draw_mic_coords(jax.random.fold_in(seeds[4], 71), 0)
    wavenumbers = jnp.clip(jnp.exp(math.log(150.0) - 2.014903 * jax.random.uniform(seeds[2], (BINS,), jnp.float32) ** shard_levels(seeds[2], (BINS,), ((0, 4),), -0.2, 0.2)), 20.0, 150.0)
    pressures = normal_values(seeds[3], (BINS, 2, SNAPS, MICS), 1.0, 6.0, ((0, 4), (3, 4)), jnp.float32)
    return dict(grid_points=grid_points, mic_coords=mic_coords, wavenumbers=wavenumbers, pressures=pressures)


def steering_tiles(points, mic_coords, wave_number, norm_scale):
    dist_x = points[0][:, None] - mic_coords[0][None, :]
    dist_y = points[1][:, None] - mic_coords[1][None, :]
    dist_z = points[2][:, None] - mic_coords[2][None, :]
    radius = jnp.sqrt(dist_x * dist_x + dist_y * dist_y + dist_z * dist_z)
    amplitude = norm_scale / radius
    phase_angle = wave_number * radius
    cos_tile = (jnp.cos(phase_angle) * amplitude).astype(jnp.bfloat16)
    sin_tile = (jnp.sin(phase_angle) * amplitude).astype(jnp.bfloat16)
    return (cos_tile, sin_tile)

def apply_forward(direction, grid_points, mic_coords, wavenumbers):
    snap_count = direction.shape[2]
    blocks = GRID // GRID_DEV
    rounded = direction.astype(jnp.bfloat16).reshape(BINS, 2 * snap_count, blocks, GRID_DEV).transpose(0, 2, 1, 3)
    point_blocks = grid_points.reshape(3, blocks, GRID_DEV).transpose(1, 0, 2)
    norm_scale = 1.0 / math.sqrt(GRID)

    def one_bin(bin_items):
        wave_number, bin_blocks = bin_items

        def add_block(totals, block_items):
            points, block_piece = block_items
            cos_tile, sin_tile = steering_tiles(points, mic_coords, wave_number, norm_scale)
            cos_sum = totals[0] + jnp.dot(block_piece, cos_tile, preferred_element_type=jnp.float32)
            sin_sum = totals[1] + jnp.dot(block_piece, sin_tile, preferred_element_type=jnp.float32)
            return ((cos_sum, sin_sum), None)
        zero_rows = jnp.zeros((2 * snap_count, MICS), jnp.float32)
        sums, unused = lax.scan(add_block, (zero_rows, zero_rows), (point_blocks, bin_blocks))
        cos_sum, sin_sum = sums
        real_part = cos_sum[:snap_count] + sin_sum[snap_count:]
        imag_part = cos_sum[snap_count:] - sin_sum[:snap_count]
        return jnp.stack([real_part, imag_part])
    return lax.map(one_bin, (wavenumbers, rounded))

def apply_adjoint(residual, grid_points, mic_coords, wavenumbers):
    snap_count = residual.shape[2]
    blocks = GRID // GRID_DEV
    rounded = residual.astype(jnp.bfloat16).reshape(BINS, 2 * snap_count, MICS)
    point_blocks = grid_points.reshape(3, blocks, GRID_DEV).transpose(1, 0, 2)
    norm_scale = 1.0 / math.sqrt(GRID)

    def one_bin(bin_items):
        wave_number, bin_rows = bin_items

        def one_block(points):
            cos_tile, sin_tile = steering_tiles(points, mic_coords, wave_number, norm_scale)
            cos_sum = lax.dot_general(bin_rows, cos_tile, (((1,), (1,)), ((), ())), preferred_element_type=jnp.float32)
            sin_sum = lax.dot_general(bin_rows, sin_tile, (((1,), (1,)), ((), ())), preferred_element_type=jnp.float32)
            real_part = cos_sum[:snap_count] - sin_sum[snap_count:]
            imag_part = cos_sum[snap_count:] + sin_sum[:snap_count]
            return jnp.stack([real_part, imag_part])
        block_images = lax.map(one_block, point_blocks)
        return block_images.transpose(1, 2, 0, 3).reshape(2, snap_count, GRID)
    return lax.map(one_bin, (wavenumbers, rounded))

def reference(grid_points, mic_coords, wavenumbers, pressures):
    residual = pressures
    gradient = apply_adjoint(residual, grid_points, mic_coords, wavenumbers)
    direction = gradient
    grad_norm = jnp.sum(gradient * gradient)
    solution = jnp.zeros_like(gradient)
    for iteration in range(ITERS):
        image = apply_forward(direction, grid_points, mic_coords, wavenumbers)
        image_norm = jnp.sum(image * image)
        step_size = grad_norm / image_norm
        solution = solution + step_size * direction
        residual = residual - step_size * image
        if iteration + 1 < ITERS:
            gradient = apply_adjoint(residual, grid_points, mic_coords, wavenumbers)
            next_norm = jnp.sum(gradient * gradient)
            direction = gradient + next_norm / grad_norm * direction
            grad_norm = next_norm
    return (solution, residual)
```

```python
import functools
import math

import jax
import jax.numpy as jnp
from jax import lax
from jax.experimental import pallas as pl
from jax.experimental.pallas import tpu as pltpu
from jax.sharding import PartitionSpec as P

F32, BF16 = jnp.float32, jnp.bfloat16
SIN_POLY = (4.442883014678955, -7.308245658874512, 3.6063544750213623, -0.8461129069328308, 0.10982698947191238)
COS_POLY = (1.4142135381698608, -6.978850841522217, 5.7394609451293945, -1.8835630416870117, 0.31069818139076233)
ROUNDER = 12582912.0
ROWS, LANES, UNROLL = 32, 256, 2
STEP = 128


def steering(gx, gy, gz, mx, my, mz, turns):
    dx, dy, dz = gx - mx, gy - my, gz - mz
    square = dx * dx + dy * dy + dz * dz
    inverse = lax.rsqrt(square)
    cycles = (square * inverse) * turns
    part = cycles - ((cycles + ROUNDER) - ROUNDER)
    t = part * part
    s = SIN_POLY[4]
    c = COS_POLY[4]
    for k in (3, 2, 1, 0):
        s = s * t + SIN_POLY[k]
        c = c * t + COS_POLY[k]
    s = s * part
    scaled = s * inverse
    return (inverse - scaled * s).astype(BF16), (scaled * c).astype(BF16)


def dot_nt(a, b):
    return lax.dot_general(a, b, (((1,), (1,)), ((), ())), preferred_element_type=F32)


def dot_nn(a, b):
    return lax.dot_general(a, b, (((1,), (0,)), ((), ())), preferred_element_type=F32)


def store_image(out_ref, image, scale):
    for s in range(out_ref.shape[2]):
        for c in range(8):
            for h in range(2):
                lo = s * 1024 + c * 128
                out_ref[c, h, s] = image[h * 16 : h * 16 + 16, lo : lo + 128] * scale


def lane_sums(x):
    return jnp.sum(x, axis=0, keepdims=True)


def first_kernel(scale, turns_ref, grid_ref, p0, p1, p2, p3, cos_ref, sin_ref, grad_ref, image_ref, wc, ws, image):
    step = pl.program_id(0)
    packs = (p0, p1, p2, p3)

    @pl.when(step == 0)
    def _():
        for s in range(4):
            w = packs[s][0:32, :].astype(BF16)
            cols = slice(s * 1024, s * 1024 + 1024)
            wc[:, cols] = w
            ws[0:16, cols] = -w[16:32]
            ws[16:32, cols] = w[0:16]
        image[...] = jnp.zeros_like(image)

    turns = turns_ref[0]
    for s in range(4):

        def rows(i, carry, s=s):
            r0 = pl.multiple_of(i * ROWS, ROWS)
            g = [jnp.broadcast_to(grid_ref[pl.ds(r0, ROWS), d : d + 1], (ROWS, LANES)) for d in range(3)]

            def lanes(j, carry):
                for q in range(UNROLL):
                    l0 = pl.multiple_of((j * UNROLL + q) * LANES, LANES)
                    m = [packs[s][32 + d : 33 + d, pl.ds(l0, LANES)] for d in range(3)]
                    c, sn = steering(*g, *m, turns)
                    o0 = pl.multiple_of(l0 + s * 1024, LANES)
                    cos_ref[pl.ds(r0, ROWS), pl.ds(o0, LANES)] = c
                    sin_ref[pl.ds(r0, ROWS), pl.ds(o0, LANES)] = sn
                return carry

            return lax.fori_loop(0, 1024 // (LANES * UNROLL), lanes, carry)

        lax.fori_loop(0, STEP // ROWS, rows, 0)

    grad = (dot_nt(wc[...], cos_ref[...]) + dot_nt(ws[...], sin_ref[...])) * scale
    grad_ref[...] = grad
    v = grad.astype(BF16)
    v2 = jnp.concatenate([v[16:32], -v[0:16]], axis=0)
    image[...] += dot_nn(v, cos_ref[...]) + dot_nn(v2, sin_ref[...])

    @pl.when(step == pl.num_programs(0) - 1)
    def _():
        store_image(image_ref, image, scale)


def second_kernel(scale, q_ref, cos_ref, sin_ref, grad0_ref, grad_ref, image_ref, sums_ref, wc, ws, image):
    step = pl.program_id(0)

    @pl.when(step == 0)
    def _():
        for s in range(4):
            for c in range(8):
                cols = slice(s * 1024 + c * 128, s * 1024 + c * 128 + 128)
                real, imag = q_ref[2 * c, s], q_ref[2 * c + 1, s]
                wc[0:16, cols] = real
                wc[16:32, cols] = imag
                ws[0:16, cols] = -imag
                ws[16:32, cols] = real
        image[...] = jnp.zeros_like(image)
        sums_ref[...] = jnp.zeros_like(sums_ref)

    grad = (dot_nt(wc[...], cos_ref[...]) + dot_nt(ws[...], sin_ref[...])) * scale
    grad_ref[...] = grad
    g0 = grad0_ref[...]
    sums_ref[0:1] += lane_sums(g0 * g0)
    sums_ref[1:2] += lane_sums(g0 * grad)
    sums_ref[2:3] += lane_sums(grad * grad)
    v = grad.astype(BF16)
    v2 = jnp.concatenate([v[16:32], -v[0:16]], axis=0)
    image[...] += dot_nn(v, cos_ref[...]) + dot_nn(v2, sin_ref[...])

    @pl.when(step == pl.num_programs(0) - 1)
    def _():
        store_image(image_ref, image, scale)


def gather_kernel(parts_ref, shard_ref, copies_ref):
    total = parts_ref[0]
    for j in range(1, 16):
        total += parts_ref[j]
    shard_ref[...] = total
    low = total.astype(BF16)
    for j in range(16):
        copies_ref[j] = low


def spread_kernel(mic_ref, parts_ref, q_ref, sums_ref, out_ref, shard):
    total = parts_ref[0]
    for j in range(1, 16):
        total += parts_ref[j]
    shard[...] = total
    q = q_ref[...]
    flat = lambda x: lane_sums(x.reshape(64, 128))
    sums = jnp.concatenate(
        [sums_ref[0:3], flat(q * q), flat(q * total), flat(total * total), jnp.zeros((2, 128), F32)], axis=0
    )
    for t in range(4):
        s = lax.rem(t + 4 - mic_ref[0], 4)
        a, b = q_ref[s], shard[s]
        for j in range(16):
            out_ref[j * 4 + t, 0:16] = a
            out_ref[j * 4 + t, 16:32] = b
            out_ref[j * 4 + t, 32:40] = sums


def local_sums_kernel(recv_ref, out_ref):
    total = recv_ref[0, 32:40]
    for j in range(1, 64):
        total += recv_ref[j, 32:40]
    out_ref[...] = total


def last_kernel(mic_ref, sums_ref, recv_ref, press_ref, h0, h1, h2, h3, x_ref, r_ref):
    total = jnp.sum(sums_ref[...], axis=1, keepdims=True)
    gg, gh, hh, qq, qp, pp = [total[i : i + 1] for i in range(6)]
    step0 = gg / qq
    norm1 = gg - 2.0 * step0 * gh + step0 * step0 * hh
    ratio = norm1 / gg
    image1 = (1.0 + ratio) * (1.0 + ratio) * qq - 2.0 * (1.0 + ratio) * step0 * qp + step0 * step0 * pp
    step1 = norm1 / image1
    lead = jnp.broadcast_to(step0 + step1 * (1.0 + ratio), (16, 128))
    tail = jnp.broadcast_to(step0 * step1, (16, 128))
    for s, hop in enumerate((h0, h1, h2, h3)):
        bin_at = lax.rem(mic_ref[0] + s, 4)
        for h in range(2):
            for c in range(8):
                rows, cols = slice(h * 16, h * 16 + 16), slice(c * 128, c * 128 + 128)
                x_ref[bin_at, h, :, cols] = lead * hop[0, rows, cols] - tail * hop[1, rows, cols]
    for m in range(4):
        for h in range(2):
            for c in range(8):
                cols = slice(c * 128, c * 128 + 128)
                j = (2 * c + h) * 4 + m
                r_ref[m, h, :, cols] = (
                    press_ref[m, h, :, cols] - lead * recv_ref[j, 0:16] + tail * recv_ref[j, 16:32]
                )


VM = pl.BlockSpec(memory_space=pltpu.VMEM)
SM = pl.BlockSpec(memory_space=pltpu.SMEM)
PARAMS = pltpu.CompilerParams(vmem_limit_bytes=48 << 20)


def whole(shape):
    return pl.BlockSpec(shape, lambda i: (0,) * len(shape))


def ahead(x, shift):
    return lax.ppermute(x, "mic", [((t + shift) % 4, t) for t in range(4)])


def body(grid_points, mic_coords, wavenumbers, pressures):
    grid_total = grid_points.shape[1] * lax.axis_size("grid")
    scale = 1.0 / math.sqrt(grid_total)
    mic = lax.axis_index("mic")
    mic_one = jnp.reshape(mic, (1,)).astype(jnp.int32)
    turns = lax.dynamic_slice(wavenumbers, (mic,), (1,)) * (0.5 / math.pi)
    flat = pressures.reshape(4, 32, 1024)
    coords = jnp.pad(mic_coords, ((0, 5), (0, 0)))

    def pack(owner):
        return jnp.concatenate([lax.dynamic_index_in_dim(flat, owner, 0, False), coords], axis=0)

    packs = [pack(mic)] + [ahead(pack(lax.rem(mic + 4 - s, 4)), s) for s in (1, 2, 3)]

    tile = jax.ShapeDtypeStruct((1024, 4096), BF16)
    tile_spec = pl.BlockSpec((STEP, 4096), lambda i: (i, 0))
    grad_type = jax.ShapeDtypeStruct((32, 1024), F32)
    grad_spec = pl.BlockSpec((32, STEP), lambda i: (0, i))
    image_type = jax.ShapeDtypeStruct((8, 2, 4, 16, 128), F32)
    scratch = [pltpu.VMEM((32, 4096), BF16), pltpu.VMEM((32, 4096), BF16), pltpu.VMEM((32, 4096), F32)]
    cos_tile, sin_tile, grad0, part0 = pl.pallas_call(
        functools.partial(first_kernel, scale),
        grid=(1024 // STEP,),
        in_specs=[SM, pl.BlockSpec((STEP, 3), lambda i: (i, 0))] + [whole((40, 1024))] * 4,
        out_specs=[tile_spec, tile_spec, grad_spec, whole(image_type.shape)],
        out_shape=[tile, tile, grad_type, image_type],
        scratch_shapes=scratch,
        compiler_params=PARAMS,
        name="build",
    )(turns, grid_points.T, *packs)

    parts = lax.all_to_all(part0.reshape(16, 4, 16, 128), "grid", 0, 0)
    shard_type = jax.ShapeDtypeStruct((4, 16, 128), F32)
    image0, copies = pl.pallas_call(
        gather_kernel,
        in_specs=[VM],
        out_specs=[VM, VM],
        out_shape=[shard_type, jax.ShapeDtypeStruct((16, 4, 16, 128), BF16)],
        name="gather",
    )(parts)
    rounded = lax.all_to_all(copies, "grid", 0, 0)

    grad1, part1, sums = pl.pallas_call(
        functools.partial(second_kernel, scale),
        grid=(1024 // STEP,),
        in_specs=[whole((16, 4, 16, 128)), tile_spec, tile_spec, grad_spec],
        out_specs=[grad_spec, whole(image_type.shape), whole((8, 128))],
        out_shape=[grad_type, image_type, jax.ShapeDtypeStruct((8, 128), F32)],
        scratch_shapes=scratch,
        compiler_params=PARAMS,
        name="again",
    )(rounded, cos_tile, sin_tile, grad0)

    both = jnp.stack([grad0, grad1])
    hops = [both] + [ahead(both, s) for s in (1, 2, 3)]
    parts = lax.all_to_all(part1.reshape(16, 4, 16, 128), "grid", 0, 0)
    sent = pl.pallas_call(
        spread_kernel,
        in_specs=[SM, VM, VM, VM],
        out_specs=VM,
        out_shape=jax.ShapeDtypeStruct((64, 40, 128), F32),
        scratch_shapes=[pltpu.VMEM((4, 16, 128), F32)],
        name="spread",
    )(mic_one, parts, image0, sums)
    recv = lax.all_to_all(sent, ("grid", "mic"), 0, 0)
    local = pl.pallas_call(
        local_sums_kernel,
        in_specs=[VM],
        out_specs=VM,
        out_shape=jax.ShapeDtypeStruct((8, 128), F32),
        name="local_sums",
    )(recv)
    total = lax.psum(local, "bin")
    out_type = jax.ShapeDtypeStruct((4, 2, 16, 1024), F32)
    return pl.pallas_call(
        last_kernel,
        in_specs=[SM] + [VM] * 7,
        out_specs=[VM, VM],
        out_shape=[out_type, out_type],
        compiler_params=PARAMS,
        name="last",
    )(mic_one, total, recv, pressures, *hops)


def solution(mesh):
    placed = (P(None, "grid"), P(None, "mic"), P("bin"), P("bin", None, None, "mic"))
    return jax.shard_map(
        body,
        mesh=mesh,
        in_specs=placed,
        out_specs=(P("bin", None, None, "grid"), P("bin", None, None, "mic")),
        check_vma=False,
    )
```

```python
import functools
import math

import jax
import jax.numpy as jnp
from jax import lax
from jax.experimental import pallas as pl
from jax.experimental.pallas import tpu as pltpu
from jax.sharding import PartitionSpec as P

F32, BF16 = jnp.float32, jnp.bfloat16
QUARTER = (2.641753911972046, -1.0863767862319946, 0.13400563597679138, -0.0077399080619215965)
SQUARE = 2.0 * math.sqrt(2.0)
ROOT = math.sqrt(2.0)
ROWS, LANES, EDGE = 16, 256, 256
VM = pl.BlockSpec(memory_space=pltpu.VMEM)
SM = pl.BlockSpec(memory_space=pltpu.SMEM)


def steering(gx, gy, gz, mx, my, mz, turns):
    dx, dy, dz = gx - mx, gy - my, gz - mz
    square = dx * dx + dy * dy + dz * dz
    inverse = lax.rsqrt(square)
    cycles = (square * inverse) * turns
    part = cycles - jnp.round(cycles)
    t = part * part
    s = QUARTER[3]
    for k in (2, 1, 0):
        s = s * t + QUARTER[k]
    s = s * part
    q = s * s
    w = SQUARE - q
    half_sin = s * (w * lax.rsqrt(w))
    half_cos = ROOT - q
    scaled = half_sin * inverse
    return (inverse - scaled * half_sin).astype(BF16), (scaled * half_cos).astype(BF16)


def dot_nt(a, b):
    return lax.dot_general(a, b, (((1,), (1,)), ((), ())), preferred_element_type=F32)


def dot_nn(a, b):
    return lax.dot_general(a, b, (((1,), (0,)), ((), ())), preferred_element_type=F32)


def multiple(x, m):
    return x if isinstance(x, int) else pl.multiple_of(x, m)


def span(index):
    return pl.ds(multiple(index * EDGE, EDGE), EDGE)


def lane_sums(x):
    return jnp.sum(x, axis=0, keepdims=True)


def swapped(v):
    return jnp.concatenate([v[16:32], -v[0:16]], axis=0)


class Tiles:
    def __init__(self, refs):
        self.refs = refs

    def get(self, step_odd, chunk_odd):
        at = (step_odd * 2 + chunk_odd) * 2
        return self.refs[at], self.refs[at + 1]

    def build(self, grid_ref, mics, turns, half, odd, pair, chunk_odd):
        c_ref, s_ref = self.get(odd, chunk_odd)
        for block in range(EDGE // ROWS):
            rows = pl.ds(multiple((half * 2 + odd) * EDGE + block * ROWS, ROWS), ROWS)
            g = [jnp.broadcast_to(grid_ref[rows, d : d + 1], (ROWS, LANES)) for d in range(3)]
            c, s = steering(*g, *mics, turns)
            at = (pl.ds(multiple(half * EDGE + block * ROWS, ROWS), ROWS), span(pair))
            c_ref[at] = c
            s_ref[at] = s

    def adjoint(self, weights, half, odd, pair, chunk_odd):
        c_ref, s_ref = self.get(odd, chunk_odd)
        wc, ws = weights[0], weights[1]
        at = (span(half), span(pair))
        cols = span(pair)
        return dot_nt(wc[chunk_odd, :, cols], c_ref[at]) + dot_nt(ws[chunk_odd, :, cols], s_ref[at])

    def forward(self, image, v, v2, half, odd, pair, chunk_odd):
        c_ref, s_ref = self.get(odd, chunk_odd)
        at = (span(half), span(pair))
        image[chunk_odd, :, span(pair)] += dot_nn(v, c_ref[at]) + dot_nn(v2, s_ref[at])


def prepare_kernel(mic_ref, press_ref, coords_ref, points_ref, g_ref, o1, o2, o3, pad):
    for s, out in ((1, o1), (2, o2), (3, o3)):
        out[0:32] = press_ref[lax.rem(mic_ref[0] + 4 - s, 4)]
        out[32:35] = coords_ref[...]
        out[35:40] = jnp.zeros((5, 1024), F32)
    pad[0:3] = points_ref[...]
    pad[3:8] = jnp.zeros((5, 1024), F32)
    for r in range(8):
        g_ref[r * 128 : r * 128 + 128, :] = pad[:, r * 128 : r * 128 + 128].T


def set_weights(wc, ws, chunk, real, imag, scale):
    odd, cols = chunk % 2, slice((chunk // 2) * EDGE, (chunk // 2) * EDGE + EDGE)
    real, imag = real * scale, imag * scale
    wc[odd, 0:16, cols] = real
    wc[odd, 16:32, cols] = imag
    ws[odd, 0:16, cols] = -imag
    ws[odd, 16:32, cols] = real


def turns_of(mic_ref, wave_ref):
    return wave_ref[mic_ref[0]] * (0.5 / math.pi)


def own_kernel(scale, mic_ref, wave_ref, press_ref, coords_ref, grid_ref, *refs):
    tiles, grad_ref, wc, ws = Tiles(refs[:8]), refs[8], refs[9], refs[10]
    turns = turns_of(mic_ref, wave_ref)
    for chunk in range(4):
        cols = slice(chunk * EDGE, chunk * EDGE + EDGE)
        w = press_ref[mic_ref[0], :, cols].astype(BF16)
        set_weights(wc, ws, chunk, w[0:16], w[16:32], scale)

    def mics(chunk):
        return [coords_ref[d : d + 1, chunk * EDGE : chunk * EDGE + EDGE] for d in range(3)]

    def half_step(half, carry):
        late = None
        for odd in range(2):
            total = jnp.zeros((32, EDGE), F32)
            for pair in range(2):
                for chunk_odd in range(2):
                    if late is not None:
                        value = tiles.adjoint((wc, ws), half, *late)
                        if late[0] == odd:
                            total += value
                        else:
                            grad_ref[:, span(half * 2 + late[0])] = done + value
                    tiles.build(grid_ref, mics(pair * 2 + chunk_odd), turns, half, odd, pair, chunk_odd)
                    late = (odd, pair, chunk_odd)
            done = total
        grad_ref[:, span(half * 2 + 1)] = done + tiles.adjoint((wc, ws), half, *late)
        return carry

    lax.fori_loop(0, 2, half_step, 0)


def store_image(out_ref, image, first):
    for odd in range(2):
        for pair in range(image.shape[2] // EDGE):
            for piece in range(2):
                tile = (pair * 2 + odd) * 2 + piece
                s, c = tile // 8 + first, tile % 8
                lo = pair * EDGE + piece * 128
                for h in range(2):
                    out_ref[c, h, s] = image[odd, h * 16 : h * 16 + 16, lo : lo + 128]


def rest_kernel(scale, mic_ref, wave_ref, grid_ref, p1, p2, p3, head_ref, *refs):
    own, tiles = Tiles(refs[:8]), Tiles(refs[8:16])
    grad_ref, image_ref, wc, ws, near, far, coords = refs[16:]
    turns = turns_of(mic_ref, wave_ref)
    for s, pack in enumerate((p1, p2, p3)):
        for chunk in range(4):
            w = pack[0:32, chunk * EDGE : chunk * EDGE + EDGE].astype(BF16)
            set_weights(wc, ws, s * 4 + chunk, w[0:16], w[16:32], scale)
        coords[:, s * 1024 : s * 1024 + 1024] = pack[32:40]
    near[...] = jnp.zeros_like(near)
    far[...] = jnp.zeros_like(far)

    def mics(pair, chunk_odd):
        lo = pl.ds(multiple((pair * 2 + chunk_odd) * EDGE, EDGE), EDGE)
        return [coords[d : d + 1, lo] for d in range(3)]

    def one_step(half, odd, v, before):
        total = head_ref[:, span(half * 2 + odd)]

        def pair_body(pair, total, first):
            if not first:
                total += tiles.adjoint((wc, ws), half, odd, pair - 1, 1)
            if before is not None:
                tiles.forward(far, *v, *before, pair, 0)
                if first:
                    for p in range(2):
                        for o in range(2):
                            own.forward(near, *v, *before, p, o)
            tiles.build(grid_ref, mics(pair, 0), turns, half, odd, pair, 0)
            total += tiles.adjoint((wc, ws), half, odd, pair, 0)
            if before is not None:
                tiles.forward(far, *v, *before, pair, 1)
            tiles.build(grid_ref, mics(pair, 1), turns, half, odd, pair, 1)
            return total

        total = pair_body(0, total, True)
        total = lax.fori_loop(1, 6, lambda pair, total: pair_body(pair, total, False), total)
        total += tiles.adjoint((wc, ws), half, odd, 5, 1)
        grad_ref[:, span(half * 2 + odd)] = total
        v = total.astype(BF16) * scale
        return v, swapped(v)

    v = one_step(0, 0, None, None)
    v = one_step(0, 1, v, (0, 0))
    v = one_step(1, 0, v, (0, 1))
    v = one_step(1, 1, v, (1, 0))
    for p in range(2):
        for o in range(2):
            own.forward(near, *v, 1, 1, p, o)

    def tail(pair, carry):
        tiles.forward(far, *v, 1, 1, pair, 0)
        tiles.forward(far, *v, 1, 1, pair, 1)
        return carry

    lax.fori_loop(0, 6, tail, 0)
    store_image(image_ref, near, 0)
    store_image(image_ref, far, 1)


def again_kernel(scale, q_ref, grad0_ref, *refs):
    own, tiles = Tiles(refs[:8]), Tiles(refs[8:16])
    both_ref, image_ref, sums_ref, wa, wb, wc, wd, near, far = refs[16:]
    for block in range(4):
        for chunk in range(4):
            real = jnp.concatenate([q_ref[4 * chunk + 2 * p, block] for p in range(2)], axis=1)
            imag = jnp.concatenate([q_ref[4 * chunk + 2 * p + 1, block] for p in range(2)], axis=1)
            if block == 0:
                set_weights(wa, wb, chunk, real, imag, scale)
            else:
                set_weights(wc, wd, (block - 1) * 4 + chunk, real, imag, scale)
    near[...] = jnp.zeros_like(near)
    far[...] = jnp.zeros_like(far)
    sums_ref[...] = jnp.zeros_like(sums_ref)

    def forward(v, half, odd):
        for o in range(2):
            for image, (c_ref, s_ref) in ((near, own.get(odd, o)), (far, tiles.get(odd, o))):
                image[o] += dot_nn(v[0], c_ref[span(half), :]) + dot_nn(v[1], s_ref[span(half), :])

    def adjoint(half, odd):
        total = None
        for o in range(2):
            for w_c, w_s, (c_ref, s_ref) in ((wa, wb, own.get(odd, o)), (wc, wd, tiles.get(odd, o))):
                value = dot_nt(w_c[o], c_ref[span(half), :]) + dot_nt(w_s[o], s_ref[span(half), :])
                total = value if total is None else total + value
        return total

    def finish(half, odd, total):
        cols = span(half * 2 + odd)
        g0 = grad0_ref[:, cols]
        both_ref[0, :, cols] = g0
        both_ref[1, :, cols] = total
        sums_ref[0:1] += lane_sums(g0 * g0)
        sums_ref[1:2] += lane_sums(g0 * total)
        sums_ref[2:3] += lane_sums(total * total)
        v = total.astype(BF16) * scale
        return v, swapped(v)

    v = finish(0, 0, adjoint(0, 0))
    for half, odd, before in ((0, 1, (0, 0)), (1, 0, (0, 1)), (1, 1, (1, 0))):
        total = adjoint(half, odd)
        forward(v, *before)
        v = finish(half, odd, total)
    forward(v, 1, 1)
    store_image(image_ref, near, 0)
    store_image(image_ref, far, 1)


def gather_kernel(parts_ref, shard_ref, copies_ref):
    total = parts_ref[0]
    for j in range(1, 16):
        total += parts_ref[j]
    shard_ref[...] = total
    low = total.astype(BF16)
    for j in range(16):
        copies_ref[j] = low


def spread_kernel(mic_ref, parts_ref, q_ref, sums_ref, out_ref, shard):
    total = parts_ref[0]
    for j in range(1, 16):
        total += parts_ref[j]
    shard[...] = total
    q = q_ref[...]

    def flat(x):
        return lane_sums(x.reshape(64, 128))

    near = sums_ref[0:3, 0:128] + sums_ref[0:3, 128:256]
    sums = jnp.concatenate([near, flat(q * q), flat(q * total), flat(total * total), jnp.zeros((2, 128), F32)], axis=0)
    for t in range(4):
        s = lax.rem(t + 4 - mic_ref[0], 4)
        a, b = q_ref[s], shard[s]
        for k in range(4):
            out_ref[t * 4 + k, 0:16] = a
            out_ref[t * 4 + k, 16:32] = b
            out_ref[t * 4 + k, 32:40] = sums


def relay_kernel(bin_ref, recv_ref, out_ref):
    sums = recv_ref[0, 32:40]
    for j in range(1, 16):
        sums += recv_ref[j, 32:40]
    for m in range(4):
        piece = recv_ref[m * 4 + bin_ref[0], 0:32]
        for j in range(16):
            out_ref[j, m * 32 : m * 32 + 32] = piece
    for j in range(16):
        out_ref[j, 128:136] = sums


def last_kernel(mic_ref, recv_ref, press_ref, h0, h1, h2, h3, x_ref, r_ref):
    total = recv_ref[0, 128:136]
    for j in range(1, 16):
        total += recv_ref[j, 128:136]
    total = jnp.sum(total, axis=1, keepdims=True)
    gg, gh, hh, qq, qp, pp = [total[i : i + 1] for i in range(6)]
    step0 = gg / qq
    norm1 = gg - 2.0 * step0 * gh + step0 * step0 * hh
    ratio = norm1 / gg
    image1 = (1.0 + ratio) * (1.0 + ratio) * qq - 2.0 * (1.0 + ratio) * step0 * qp + step0 * step0 * pp
    step1 = norm1 / image1
    lead = jnp.broadcast_to(step0 + step1 * (1.0 + ratio), (16, 128))
    tail = jnp.broadcast_to(step0 * step1, (16, 128))
    for s, hop in enumerate((h0, h1, h2, h3)):
        bin_at = lax.rem(mic_ref[0] + s, 4)
        for h in range(2):
            for c in range(8):
                rows, cols = slice(h * 16, h * 16 + 16), slice(c * 128, c * 128 + 128)
                x_ref[bin_at, h, :, cols] = lead * hop[0, rows, cols] - tail * hop[1, rows, cols]
    for m in range(4):
        for h in range(2):
            for c in range(8):
                cols = slice(c * 128, c * 128 + 128)
                q = recv_ref[2 * c + h, m * 32 : m * 32 + 16]
                p = recv_ref[2 * c + h, m * 32 + 16 : m * 32 + 32]
                r_ref[m, h, :, cols] = press_ref[m, h, :, cols] - lead * q + tail * p


def call(kernel, name, in_specs, out_shape, scratch=(), limit=16):
    return pl.pallas_call(
        kernel,
        in_specs=in_specs,
        out_specs=jax.tree.map(lambda _: VM, out_shape),
        out_shape=out_shape,
        scratch_shapes=list(scratch),
        compiler_params=pltpu.CompilerParams(vmem_limit_bytes=limit << 20),
        name=name,
    )


def array(*shape, dtype=F32):
    return jax.ShapeDtypeStruct(shape, dtype)


def ahead(x, shift):
    return lax.ppermute(x, "mic", [((t + shift) % 4, t) for t in range(4)])


def body(grid_points, mic_coords, wavenumbers, pressures):
    scale = 1.0 / math.sqrt(grid_points.shape[1] * lax.axis_size("grid"))
    mic = jnp.reshape(lax.axis_index("mic"), (1,)).astype(jnp.int32)
    bin_at = jnp.reshape(lax.axis_index("bin"), (1,)).astype(jnp.int32)
    flat = pressures.reshape(4, 32, 1024)

    points, *packs = call(
        prepare_kernel, "prepare", [SM, VM, VM, VM], [array(1024, 8)] + [array(40, 1024)] * 3, [pltpu.VMEM((8, 1024), F32)]
    )(mic, flat, mic_coords, grid_points)
    packs = [ahead(pack, s) for s, pack in zip((1, 2, 3), packs)]

    def held(width):
        return [pltpu.VMEM((512, width), BF16)] * 8

    weights_near = [pltpu.VMEM((2, 32, 512), BF16)] * 2
    weights_far = [pltpu.VMEM((2, 32, 1536), BF16)] * 2
    images = [pltpu.VMEM((2, 32, 512), F32), pltpu.VMEM((2, 32, 1536), F32)]
    *near, head = call(
        functools.partial(own_kernel, scale), "own", [SM, SM, VM, VM, VM], held(512) + [array(32, 1024)], weights_near
    )(mic, wavenumbers, flat, mic_coords, points)
    near = [pltpu.with_memory_space_constraint(t, pltpu.VMEM) for t in near]
    image_type = array(8, 2, 4, 16, 128)
    *far, grad0, part0 = call(
        functools.partial(rest_kernel, scale),
        "rest",
        [SM, SM] + [VM] * 13,
        held(1536) + [array(32, 1024), image_type],
        weights_far + images + [pltpu.VMEM((8, 3072), F32)],
        limit=32,
    )(mic, wavenumbers, points, *packs, head, *near)
    far = [pltpu.with_memory_space_constraint(t, pltpu.VMEM) for t in far]

    parts = lax.all_to_all(part0.reshape(16, 4, 16, 128), "grid", 0, 0)
    image0, copies = call(
        gather_kernel, "gather", [VM], [array(4, 16, 128), array(16, 4, 16, 128, dtype=BF16)]
    )(parts)
    rounded = lax.all_to_all(copies, "grid", 0, 0)

    both, part1, sums = call(
        functools.partial(again_kernel, scale),
        "again",
        [VM] * 18,
        [array(2, 32, 1024), image_type, array(8, EDGE)],
        weights_near + weights_far + images,
        limit=32,
    )(rounded, grad0, *near, *far)

    hops = [both] + [ahead(both, s) for s in (1, 2, 3)]
    parts = lax.all_to_all(part1.reshape(16, 4, 16, 128), "grid", 0, 0)
    sent = call(spread_kernel, "spread", [SM, VM, VM, VM], array(16, 40, 128), [pltpu.VMEM((4, 16, 128), F32)])(
        mic, parts, image0, sums
    )
    recv = lax.all_to_all(sent, ("mic", "bin"), 0, 0)
    sent = call(relay_kernel, "relay", [SM, VM], array(16, 136, 128))(bin_at, recv)
    recv = lax.all_to_all(sent, "grid", 0, 0)
    out_type = array(4, 2, 16, 1024)
    return call(last_kernel, "last", [SM] + [VM] * 6, [out_type, out_type])(mic, recv, pressures, *hops)


def solution(mesh):
    placed = (P(None, "grid"), P(None, "mic"), P("bin"), P("bin", None, None, "mic"))
    return jax.shard_map(
        body,
        mesh=mesh,
        in_specs=placed,
        out_specs=(P("bin", None, None, "grid"), P("bin", None, None, "mic")),
        check_vma=False,
    )
```

```python
import functools
import math

import jax
import jax.numpy as jnp
from jax import lax
from jax.experimental import pallas as pl
from jax.experimental.pallas import tpu as pltpu
from jax.sharding import PartitionSpec as P

F32, BF16 = jnp.float32, jnp.bfloat16
QUARTER = (2.641753911972046, -1.0863767862319946, 0.13400563597679138, -0.0077399080619215965)
SQUARE = 2.0 * math.sqrt(2.0)
ROOT = math.sqrt(2.0)
ROWS, LANES, EDGE = 16, 256, 256
VM = pl.BlockSpec(memory_space=pltpu.VMEM)
SM = pl.BlockSpec(memory_space=pltpu.SMEM)
ANY = pl.BlockSpec(memory_space=pl.ANY)
HBM = pl.BlockSpec(memory_space=pltpu.HBM)


def steering(gx, gy, gz, mx, my, mz, turns):
    dx, dy, dz = gx - mx, gy - my, gz - mz
    square = dx * dx + dy * dy + dz * dz
    inverse = lax.rsqrt(square)
    cycles = (square * inverse) * turns
    part = cycles - jnp.round(cycles)
    t = part * part
    s = QUARTER[3]
    for k in (2, 1, 0):
        s = s * t + QUARTER[k]
    s = s * part
    q = s * s
    w = SQUARE - q
    half_sin = s * (w * lax.rsqrt(w))
    half_cos = ROOT - q
    scaled = half_sin * inverse
    return (inverse - scaled * half_sin).astype(BF16), (scaled * half_cos).astype(BF16)


def dot_nt(a, b):
    return lax.dot_general(a, b, (((1,), (1,)), ((), ())), preferred_element_type=F32)


def dot_nn(a, b):
    return lax.dot_general(a, b, (((1,), (0,)), ((), ())), preferred_element_type=F32)


def multiple(x, m):
    return x if isinstance(x, int) else pl.multiple_of(x, m)


def span(index):
    return pl.ds(multiple(index * EDGE, EDGE), EDGE)


def lane_sums(x):
    return jnp.sum(x, axis=0, keepdims=True)


def swapped(v):
    return jnp.concatenate([v[16:32], -v[0:16]], axis=0)


class Tiles:
    def __init__(self, refs):
        self.refs = refs

    def get(self, step_odd, chunk_odd):
        at = (step_odd * 2 + chunk_odd) * 2
        return self.refs[at], self.refs[at + 1]

    def build(self, grid_ref, mics, turns, half, odd, pair, chunk_odd):
        c_ref, s_ref = self.get(odd, chunk_odd)
        for block in range(EDGE // ROWS):
            rows = pl.ds(multiple((half * 2 + odd) * EDGE + block * ROWS, ROWS), ROWS)
            g = [jnp.broadcast_to(grid_ref[rows, d : d + 1], (ROWS, LANES)) for d in range(3)]
            c, s = steering(*g, *mics, turns)
            at = (pl.ds(multiple(half * EDGE + block * ROWS, ROWS), ROWS), span(pair))
            c_ref[at] = c
            s_ref[at] = s

    def adjoint(self, weights, half, odd, pair, chunk_odd):
        c_ref, s_ref = self.get(odd, chunk_odd)
        wc, ws = weights[0], weights[1]
        at = (span(half), span(pair))
        cols = span(pair)
        return dot_nt(wc[chunk_odd, :, cols], c_ref[at]) + dot_nt(ws[chunk_odd, :, cols], s_ref[at])

    def forward(self, image, v, v2, half, odd, pair, chunk_odd):
        c_ref, s_ref = self.get(odd, chunk_odd)
        at = (span(half), span(pair))
        image[chunk_odd, :, span(pair)] += dot_nn(v, c_ref[at]) + dot_nn(v2, s_ref[at])


def three(x):
    high = x.astype(BF16).astype(F32)
    left = x - high
    middle = left.astype(BF16).astype(F32)
    return high, middle, (left - middle).astype(BF16).astype(F32)


def prepare_kernel(mic_ref, wave_hbm, press_hbm, coords_hbm, points_hbm, g_ref, turns_ref, p0, p1, p2, p3, *scratch):
    wave_ref, press, coords, pad, sems = scratch
    copies = [
        pltpu.make_async_copy(press_hbm, press, sems.at[0]),
        pltpu.make_async_copy(coords_hbm, coords, sems.at[1]),
        pltpu.make_async_copy(points_hbm, pad.at[0:3], sems.at[2]),
        pltpu.make_async_copy(wave_hbm, wave_ref, sems.at[3]),
    ]
    for copy in copies:
        copy.start()
    for copy in copies:
        copy.wait()
    turns_ref[...] = jnp.full((8, 128), wave_ref[mic_ref[0]] * (0.5 / math.pi), F32)
    high, middle, low = [part.astype(BF16) for part in three(coords[...])]
    for s, out in enumerate((p0, p1, p2, p3)):
        out[0:32] = press[lax.rem(mic_ref[0] + 4 - s, 4)].astype(BF16)
        out[32:35], out[35:38], out[38:41] = high, middle, low
        out[41:48] = jnp.zeros((7, 1024), BF16)
    pad[3:8] = jnp.zeros((5, 1024), F32)
    for r in range(8):
        g_ref[r * 128 : r * 128 + 128, :] = pad[:, r * 128 : r * 128 + 128].T


def whole_coords(pack):
    parts = pack[32:48].astype(F32)
    return (parts[0:3] + parts[3:6]) + parts[6:9]


def set_weights(wc, ws, chunk, real, imag, scale):
    odd, cols = chunk % 2, slice((chunk // 2) * EDGE, (chunk // 2) * EDGE + EDGE)
    real, imag = real * scale, imag * scale
    wc[odd, 0:16, cols] = real
    wc[odd, 16:32, cols] = imag
    ws[odd, 0:16, cols] = -imag
    ws[odd, 16:32, cols] = real


def own_kernel(scale, pack, turns_ref, grid_ref, *refs):
    tiles, grad_ref, wc, ws, coords = Tiles(refs[:8]), refs[8], refs[9], refs[10], refs[11]
    turns = turns_ref[0:1, 0:1]
    for chunk in range(4):
        w = pack[0:32, chunk * EDGE : chunk * EDGE + EDGE]
        set_weights(wc, ws, chunk, w[0:16], w[16:32], scale)
    coords[0:3] = whole_coords(pack)

    def mics(chunk):
        return [coords[d : d + 1, chunk * EDGE : chunk * EDGE + EDGE] for d in range(3)]

    def half_step(half, carry):
        late = None
        for odd in range(2):
            total = jnp.zeros((32, EDGE), F32)
            for pair in range(2):
                for chunk_odd in range(2):
                    if late is not None:
                        value = tiles.adjoint((wc, ws), half, *late)
                        if late[0] == odd:
                            total += value
                        else:
                            grad_ref[:, span(half * 2 + late[0])] = done + value
                    tiles.build(grid_ref, mics(pair * 2 + chunk_odd), turns, half, odd, pair, chunk_odd)
                    late = (odd, pair, chunk_odd)
            done = total
        grad_ref[:, span(half * 2 + 1)] = done + tiles.adjoint((wc, ws), half, *late)
        return carry

    lax.fori_loop(0, 2, half_step, 0)


def store_image(out_ref, image, first):
    for odd in range(2):
        for pair in range(image.shape[2] // EDGE):
            for piece in range(2):
                tile = (pair * 2 + odd) * 2 + piece
                s, c = tile // 8 + first, tile % 8
                lo = pair * EDGE + piece * 128
                for h in range(2):
                    out_ref[c, h, s] = image[odd, h * 16 : h * 16 + 16, lo : lo + 128]


def rest_kernel(scale, turns_ref, grid_ref, p1, p2, p3, head_ref, *refs):
    own, tiles = Tiles(refs[:8]), Tiles(refs[8:16])
    grad_ref, image_ref, wc, ws, near, far, coords = refs[16:]
    turns = turns_ref[0:1, 0:1]
    for s, pack in enumerate((p1, p2, p3)):
        for chunk in range(4):
            w = pack[0:32, chunk * EDGE : chunk * EDGE + EDGE]
            set_weights(wc, ws, s * 4 + chunk, w[0:16], w[16:32], scale)
        coords[0:3, s * 1024 : s * 1024 + 1024] = whole_coords(pack)
    near[...] = jnp.zeros_like(near)
    far[...] = jnp.zeros_like(far)

    def mics(pair, chunk_odd):
        lo = pl.ds(multiple((pair * 2 + chunk_odd) * EDGE, EDGE), EDGE)
        return [coords[d : d + 1, lo] for d in range(3)]

    def one_step(half, odd, v, before):
        total = head_ref[:, span(half * 2 + odd)]

        def pair_body(pair, total, first):
            if not first:
                total += tiles.adjoint((wc, ws), half, odd, pair - 1, 1)
            if before is not None:
                tiles.forward(far, *v, *before, pair, 0)
                if first:
                    for p in range(2):
                        for o in range(2):
                            own.forward(near, *v, *before, p, o)
            tiles.build(grid_ref, mics(pair, 0), turns, half, odd, pair, 0)
            total += tiles.adjoint((wc, ws), half, odd, pair, 0)
            if before is not None:
                tiles.forward(far, *v, *before, pair, 1)
            tiles.build(grid_ref, mics(pair, 1), turns, half, odd, pair, 1)
            return total

        total = pair_body(0, total, True)
        total = lax.fori_loop(1, 6, lambda pair, total: pair_body(pair, total, False), total)
        total += tiles.adjoint((wc, ws), half, odd, 5, 1)
        grad_ref[:, span(half * 2 + odd)] = total
        v = total.astype(BF16) * scale
        return v, swapped(v)

    v = one_step(0, 0, None, None)
    v = one_step(0, 1, v, (0, 0))
    v = one_step(1, 0, v, (0, 1))
    v = one_step(1, 1, v, (1, 0))
    for p in range(2):
        for o in range(2):
            own.forward(near, *v, 1, 1, p, o)

    def tail(pair, carry):
        tiles.forward(far, *v, 1, 1, pair, 0)
        tiles.forward(far, *v, 1, 1, pair, 1)
        return carry

    lax.fori_loop(0, 6, tail, 0)
    store_image(image_ref, near, 0)
    store_image(image_ref, far, 1)


def again_kernel(scale, q_ref, grad0_ref, *refs):
    own, tiles = Tiles(refs[:8]), Tiles(refs[8:16])
    packed_ref, image_ref, sums_ref, wa, wb, wc, wd, near, far, grad_ref = refs[16:]
    for block in range(4):
        for chunk in range(4):
            real = jnp.concatenate([q_ref[4 * chunk + 2 * p, block] for p in range(2)], axis=1)
            imag = jnp.concatenate([q_ref[4 * chunk + 2 * p + 1, block] for p in range(2)], axis=1)
            if block == 0:
                set_weights(wa, wb, chunk, real, imag, scale)
            else:
                set_weights(wc, wd, (block - 1) * 4 + chunk, real, imag, scale)
    near[...] = jnp.zeros_like(near)
    far[...] = jnp.zeros_like(far)
    sums_ref[...] = jnp.zeros_like(sums_ref)

    def forward(v, half, odd):
        for o in range(2):
            for image, (c_ref, s_ref) in ((near, own.get(odd, o)), (far, tiles.get(odd, o))):
                image[o] += dot_nn(v[0], c_ref[span(half), :]) + dot_nn(v[1], s_ref[span(half), :])

    def adjoint(half, odd):
        total = None
        for o in range(2):
            for w_c, w_s, (c_ref, s_ref) in ((wa, wb, own.get(odd, o)), (wc, wd, tiles.get(odd, o))):
                value = dot_nt(w_c[o], c_ref[span(half), :]) + dot_nt(w_s[o], s_ref[span(half), :])
                total = value if total is None else total + value
        return total

    def finish(half, odd, total):
        cols = span(half * 2 + odd)
        g0 = grad0_ref[:, cols]
        grad_ref[:, cols] = total
        sums_ref[0:1] += lane_sums(g0 * g0)
        sums_ref[1:2] += lane_sums(g0 * total)
        sums_ref[2:3] += lane_sums(total * total)
        v = total.astype(BF16) * scale
        return v, swapped(v)

    v = finish(0, 0, adjoint(0, 0))
    for half, odd, before in ((0, 1, (0, 0)), (1, 0, (0, 1)), (1, 1, (1, 0))):
        total = adjoint(half, odd)
        forward(v, *before)
        v = finish(half, odd, total)
    forward(v, 1, 1)
    store_image(image_ref, near, 0)
    store_image(image_ref, far, 1)
    gg = jnp.sum(sums_ref[0:1], axis=1, keepdims=True)
    gh = jnp.sum(sums_ref[1:2], axis=1, keepdims=True)
    along = jnp.where(gg > 0.0, gh / jnp.where(gg > 0.0, gg, 1.0), 0.0)
    packed_ref[0:32] = grad0_ref[...].astype(BF16)
    packed_ref[32:64] = (grad_ref[...] - along * grad0_ref[...]).astype(BF16)
    high, middle, low = [jnp.broadcast_to(part, (1, 1024)) for part in three(along)]
    packed_ref[64:80] = jnp.concatenate([high, middle, low, jnp.zeros((13, 1024), F32)], axis=0).astype(BF16)


def gather_kernel(parts_ref, shard_ref, copies_ref):
    total = parts_ref[0]
    for j in range(1, 16):
        total += parts_ref[j]
    shard_ref[...] = total
    low = total.astype(BF16)
    for j in range(16):
        copies_ref[j] = low


def spread_kernel(mic_ref, parts_ref, q_ref, sums_ref, *refs):
    out_ref, shard = refs[3:]
    total = parts_ref[0]
    for j in range(1, 16):
        total += parts_ref[j]
    shard[...] = total
    q = q_ref[...]

    def flat(x):
        return lane_sums(x.reshape(64, 128))

    near = sums_ref[0:3, 0:128] + sums_ref[0:3, 128:256]
    sums = jnp.concatenate([near, flat(q * q), flat(q * total), flat(total * total), jnp.zeros((2, 128), F32)], axis=0)
    for t in range(4):
        s = lax.rem(t + 4 - mic_ref[0], 4)
        a, b = q_ref[s], shard[s]
        for k in range(4):
            out_ref[t * 4 + k, 0:16] = a
            out_ref[t * 4 + k, 16:32] = b
            out_ref[t * 4 + k, 32:40] = sums


def relay_kernel(bin_ref, recv_ref, out_ref):
    sums = recv_ref[0, 32:40]
    for j in range(1, 16):
        sums += recv_ref[j, 32:40]
    for m in range(4):
        piece = recv_ref[m * 4 + bin_ref[0], 0:32]
        for j in range(16):
            out_ref[j, m * 32 : m * 32 + 32] = piece
    for j in range(16):
        out_ref[j, 128:136] = sums


def last_kernel(mic_ref, recv_ref, press_hbm, *refs):
    packs, (x_ref, r_ref, press_ref, sem) = refs[:4], refs[4:]
    copy = pltpu.make_async_copy(press_hbm, press_ref, sem)
    copy.start()
    total = recv_ref[0, 128:136]
    for j in range(1, 16):
        total += recv_ref[j, 128:136]
    total = jnp.sum(total, axis=1, keepdims=True)
    gg, gh, hh, qq, qp, pp = [total[i : i + 1] for i in range(6)]
    step0 = gg / qq
    norm1 = gg - 2.0 * step0 * gh + step0 * step0 * hh
    ratio = norm1 / gg
    image1 = (1.0 + ratio) * (1.0 + ratio) * qq - 2.0 * (1.0 + ratio) * step0 * qp + step0 * step0 * pp
    step1 = norm1 / image1
    lead = jnp.broadcast_to(step0 + step1 * (1.0 + ratio), (16, 128))
    tail = jnp.broadcast_to(step0 * step1, (16, 128))
    for s, pack in enumerate(packs):
        bin_at = lax.rem(mic_ref[0] + s, 4)
        parts = pack[64:80, 0:128].astype(F32)
        along = (parts[0:1] + parts[1:2]) + parts[2:3]
        first = lead - tail * along
        for h in range(2):
            for c in range(8):
                cols = slice(c * 128, c * 128 + 128)
                g = pack[h * 16 : h * 16 + 16, cols].astype(F32)
                y = pack[32 + h * 16 : 48 + h * 16, cols].astype(F32)
                x_ref[bin_at, h, :, cols] = first * g - tail * y
    copy.wait()
    for m in range(4):
        for h in range(2):
            for c in range(8):
                cols = slice(c * 128, c * 128 + 128)
                q = recv_ref[2 * c + h, m * 32 : m * 32 + 16]
                p = recv_ref[2 * c + h, m * 32 + 16 : m * 32 + 32]
                r_ref[m, h, :, cols] = press_ref[m, h, :, cols] - lead * q + tail * p


def call(kernel, name, in_specs, out_shape, scratch=(), limit=4, work=0):
    return pl.pallas_call(
        kernel,
        in_specs=in_specs,
        out_specs=jax.tree.map(lambda _: VM, out_shape),
        out_shape=out_shape,
        scratch_shapes=list(scratch),
        compiler_params=pltpu.CompilerParams(vmem_limit_bytes=limit << 20),
        cost_estimate=pl.CostEstimate(flops=work, bytes_accessed=0, transcendentals=0) if work else None,
        name=name,
    )


def array(*shape, dtype=F32):
    return jax.ShapeDtypeStruct(shape, dtype)


def ahead(x, shift):
    return lax.ppermute(x, "mic", [((t + shift) % 4, t) for t in range(4)])


def body(grid_points, mic_coords, wavenumbers, pressures):
    scale = 1.0 / math.sqrt(grid_points.shape[1] * lax.axis_size("grid"))
    mic, bin_at = [jnp.reshape(lax.axis_index(name), (1,)).astype(jnp.int32) for name in ("mic", "bin")]
    flat = pressures.reshape(4, 32, 1024)

    points, turns, *packs = call(
        prepare_kernel,
        "prepare",
        [SM, HBM, HBM, HBM, HBM],
        [pltpu.VMEM((1024, 8), F32), pltpu.VMEM((8, 128), F32)] + [pltpu.VMEM((48, 1024), BF16)] * 4,
        [
            pltpu.SMEM((4,), F32),
            pltpu.VMEM((4, 32, 1024), F32),
            pltpu.VMEM((3, 1024), F32),
            pltpu.VMEM((8, 1024), F32),
            pltpu.SemaphoreType.DMA((4,)),
        ],
        limit=60,
    )(mic, wavenumbers, flat, mic_coords, grid_points)
    packs[1:] = [ahead(pack, s) for s, pack in zip((1, 2, 3), packs[1:])]

    def held(width):
        return [pltpu.VMEM((512, width), BF16)] * 8

    weights_near = [pltpu.VMEM((2, 32, 512), BF16)] * 2
    weights_far = [pltpu.VMEM((2, 32, 1536), BF16)] * 2
    images = [pltpu.VMEM((2, 32, 512), F32), pltpu.VMEM((2, 32, 1536), F32)]
    *near, head = call(
        functools.partial(own_kernel, scale),
        "own",
        [VM] * 3,
        held(512) + [array(32, 1024)],
        weights_near + [pltpu.VMEM((8, 1024), F32)],
    )(packs[0], turns, points)
    near = [pltpu.with_memory_space_constraint(t, pltpu.VMEM) for t in near]
    image_type = array(8, 2, 4, 16, 128)
    *far, grad0, part0 = call(
        functools.partial(rest_kernel, scale),
        "rest",
        [VM] * 14,
        held(1536) + [array(32, 1024), image_type],
        weights_far + images + [pltpu.VMEM((8, 3072), F32)],
    )(turns, points, *packs[1:], head, *near)
    far = [pltpu.with_memory_space_constraint(t, pltpu.VMEM) for t in far]

    parts = lax.all_to_all(part0.reshape(16, 4, 16, 128), "grid", 0, 0)
    image0, copies = call(
        gather_kernel, "gather", [VM], [array(4, 16, 128), array(16, 4, 16, 128, dtype=BF16)]
    )(parts)
    rounded = lax.all_to_all(copies, "grid", 0, 0)

    packed, part1, sums = call(
        functools.partial(again_kernel, scale),
        "again",
        [VM] * 18,
        [array(80, 1024, dtype=BF16), image_type, array(8, EDGE)],
        weights_near + weights_far + images + [pltpu.VMEM((32, 1024), F32)],
        work=8 << 30,
    )(rounded, grad0, *near, *far)

    hops = [packed] + [ahead(packed, s) for s in (1, 2, 3)]
    parts = lax.all_to_all(part1.reshape(16, 4, 16, 128), "grid", 0, 0)
    sent = call(
        spread_kernel, "spread", [SM, VM, VM, VM] + [ANY] * 3, array(16, 40, 128), [pltpu.VMEM((4, 16, 128), F32)]
    )(mic, parts, image0, sums, *hops[1:])
    recv = lax.all_to_all(sent, ("mic", "bin"), 0, 0)
    sent = call(relay_kernel, "relay", [SM, VM], array(16, 136, 128))(bin_at, recv)
    recv = lax.all_to_all(sent, "grid", 0, 0)
    out_type = array(4, 2, 16, 1024)
    return call(
        last_kernel,
        "last",
        [SM, VM, HBM] + [VM] * 4,
        [out_type, out_type],
        [pltpu.VMEM((4, 2, 16, 1024), F32), pltpu.SemaphoreType.DMA],
    )(mic, recv, pressures, *hops)


def solution(mesh):
    placed = (P(None, "grid"), P(None, "mic"), P("bin"), P("bin", None, None, "mic"))
    return jax.shard_map(
        body,
        mesh=mesh,
        in_specs=placed,
        out_specs=(P("bin", None, None, "grid"), P("bin", None, None, "mic")),
        check_vma=False,
    )
```

```python
import functools
import math

import jax
import jax.numpy as jnp
from jax import lax
from jax.experimental import pallas as pl
from jax.experimental.pallas import tpu as pltpu
from jax.sharding import PartitionSpec as P

F32, BF16 = jnp.float32, jnp.bfloat16
QUARTER = (2.641753911972046, -1.0863767862319946, 0.13400563597679138, -0.0077399080619215965)
SQUARE = 2.0 * math.sqrt(2.0)
ROOT = math.sqrt(2.0)
ROWS, LANES, EDGE = 16, 256, 256
VM = pl.BlockSpec(memory_space=pltpu.VMEM)
SM = pl.BlockSpec(memory_space=pltpu.SMEM)
ANY = pl.BlockSpec(memory_space=pl.ANY)
HBM = pl.BlockSpec(memory_space=pltpu.HBM)


def steering(gx, gy, gz, mx, my, mz, turns):
    dx, dy, dz = gx - mx, gy - my, gz - mz
    square = dx * dx + dy * dy + dz * dz
    inverse = lax.rsqrt(square)
    cycles = (square * inverse) * turns
    part = cycles - jnp.round(cycles)
    t = part * part
    s = QUARTER[3]
    for k in (2, 1, 0):
        s = s * t + QUARTER[k]
    s = s * part
    q = s * s
    w = SQUARE - q
    half_sin = s * (w * lax.rsqrt(w))
    half_cos = ROOT - q
    scaled = half_sin * inverse
    return (inverse - scaled * half_sin).astype(BF16), (scaled * half_cos).astype(BF16)


def dot_nt(a, b):
    return lax.dot_general(a, b, (((1,), (1,)), ((), ())), preferred_element_type=F32)


def dot_nn(a, b):
    return lax.dot_general(a, b, (((1,), (0,)), ((), ())), preferred_element_type=F32)


def multiple(x, m):
    return x if isinstance(x, int) else pl.multiple_of(x, m)


def span(index):
    return pl.ds(multiple(index * EDGE, EDGE), EDGE)


def lane_sums(x):
    return jnp.sum(x, axis=0, keepdims=True)


def swapped(v):
    return jnp.concatenate([v[16:32], -v[0:16]], axis=0)


class Tiles:
    def __init__(self, refs):
        self.refs = refs

    def get(self, step_odd, chunk_odd):
        at = (step_odd * 2 + chunk_odd) * 2
        return self.refs[at], self.refs[at + 1]

    def build(self, grid_ref, mics, turns, half, odd, pair, chunk_odd):
        c_ref, s_ref = self.get(odd, chunk_odd)
        for block in range(EDGE // ROWS):
            rows = pl.ds(multiple((half * 2 + odd) * EDGE + block * ROWS, ROWS), ROWS)
            g = [jnp.broadcast_to(grid_ref[rows, d : d + 1], (ROWS, LANES)) for d in range(3)]
            c, s = steering(*g, *mics, turns)
            at = (pl.ds(multiple(half * EDGE + block * ROWS, ROWS), ROWS), span(pair))
            c_ref[at] = c
            s_ref[at] = s

    def adjoint(self, weights, half, odd, pair, chunk_odd):
        c_ref, s_ref = self.get(odd, chunk_odd)
        wc, ws = weights[0], weights[1]
        at = (span(half), span(pair))
        cols = span(pair)
        return dot_nt(wc[chunk_odd, :, cols], c_ref[at]) + dot_nt(ws[chunk_odd, :, cols], s_ref[at])

    def forward(self, image, v, v2, half, odd, pair, chunk_odd):
        c_ref, s_ref = self.get(odd, chunk_odd)
        at = (span(half), span(pair))
        image[chunk_odd, :, span(pair)] += dot_nn(v, c_ref[at]) + dot_nn(v2, s_ref[at])


def three(x):
    high = x.astype(BF16).astype(F32)
    left = x - high
    middle = left.astype(BF16).astype(F32)
    return high, middle, (left - middle).astype(BF16).astype(F32)


def prepare_kernel(mic_ref, wave_hbm, press_hbm, coords_hbm, points_hbm, g_ref, turns_ref, p0, p1, p2, p3, *scratch):
    wave_ref, press, coords, pad, sems = scratch
    copies = [
        pltpu.make_async_copy(press_hbm, press, sems.at[0]),
        pltpu.make_async_copy(coords_hbm, coords, sems.at[1]),
        pltpu.make_async_copy(points_hbm, pad.at[0:3], sems.at[2]),
        pltpu.make_async_copy(wave_hbm, wave_ref, sems.at[3]),
    ]
    for copy in copies:
        copy.start()
    for copy in copies:
        copy.wait()
    turns_ref[...] = jnp.full((8, 128), wave_ref[mic_ref[0]] * (0.5 / math.pi), F32)
    high, middle, low = [part.astype(BF16) for part in three(coords[...])]
    for s, out in enumerate((p0, p1, p2, p3)):
        out[0:32] = press[lax.rem(mic_ref[0] + 4 - s, 4)].astype(BF16)
        out[32:35], out[35:38], out[38:41] = high, middle, low
        out[41:48] = jnp.zeros((7, 1024), BF16)
    pad[3:8] = jnp.zeros((5, 1024), F32)
    for r in range(8):
        g_ref[r * 128 : r * 128 + 128, :] = pad[:, r * 128 : r * 128 + 128].T


def whole_coords(pack):
    parts = pack[32:48].astype(F32)
    return (parts[0:3] + parts[3:6]) + parts[6:9]


def set_weights(wc, ws, chunk, real, imag, scale):
    odd, cols = chunk % 2, slice((chunk // 2) * EDGE, (chunk // 2) * EDGE + EDGE)
    real, imag = real * scale, imag * scale
    wc[odd, 0:16, cols] = real
    wc[odd, 16:32, cols] = imag
    ws[odd, 0:16, cols] = -imag
    ws[odd, 16:32, cols] = real


def own_kernel(scale, pack, turns_ref, grid_ref, *refs):
    tiles, grad_ref, wc, ws, coords = Tiles(refs[:8]), refs[8], refs[9], refs[10], refs[11]
    turns = turns_ref[0:1, 0:1]
    for chunk in range(4):
        w = pack[0:32, chunk * EDGE : chunk * EDGE + EDGE]
        set_weights(wc, ws, chunk, w[0:16], w[16:32], scale)
    coords[0:3] = whole_coords(pack)

    def mics(chunk):
        return [coords[d : d + 1, chunk * EDGE : chunk * EDGE + EDGE] for d in range(3)]

    def half_step(half, carry):
        late = None
        for odd in range(2):
            total = jnp.zeros((32, EDGE), F32)
            for pair in range(2):
                for chunk_odd in range(2):
                    if late is not None:
                        value = tiles.adjoint((wc, ws), half, *late)
                        if late[0] == odd:
                            total += value
                        else:
                            grad_ref[:, span(half * 2 + late[0])] = done + value
                    tiles.build(grid_ref, mics(pair * 2 + chunk_odd), turns, half, odd, pair, chunk_odd)
                    late = (odd, pair, chunk_odd)
            done = total
        grad_ref[:, span(half * 2 + 1)] = done + tiles.adjoint((wc, ws), half, *late)
        return carry

    lax.fori_loop(0, 2, half_step, 0)


def store_image(out_ref, image, first):
    for odd in range(2):
        for pair in range(image.shape[2] // EDGE):
            for piece in range(2):
                tile = (pair * 2 + odd) * 2 + piece
                s, c = tile // 8 + first, tile % 8
                lo = pair * EDGE + piece * 128
                for h in range(2):
                    out_ref[c, h, s] = image[odd, h * 16 : h * 16 + 16, lo : lo + 128].astype(BF16)


def rest_kernel(scale, turns_ref, grid_ref, p1, p2, p3, head_ref, *refs):
    own, tiles = Tiles(refs[:8]), Tiles(refs[8:16])
    grad_ref, image_ref, wc, ws, near, far, coords = refs[16:]
    turns = turns_ref[0:1, 0:1]
    for s, pack in enumerate((p1, p2, p3)):
        for chunk in range(4):
            w = pack[0:32, chunk * EDGE : chunk * EDGE + EDGE]
            set_weights(wc, ws, s * 4 + chunk, w[0:16], w[16:32], scale)
        coords[0:3, s * 1024 : s * 1024 + 1024] = whole_coords(pack)
    near[...] = jnp.zeros_like(near)
    far[...] = jnp.zeros_like(far)

    def mics(pair, chunk_odd):
        lo = pl.ds(multiple((pair * 2 + chunk_odd) * EDGE, EDGE), EDGE)
        return [coords[d : d + 1, lo] for d in range(3)]

    def one_step(half, odd, v, before):
        total = head_ref[:, span(half * 2 + odd)]

        def pair_body(pair, total, first):
            if not first:
                total += tiles.adjoint((wc, ws), half, odd, pair - 1, 1)
            if before is not None:
                tiles.forward(far, *v, *before, pair, 0)
                if first:
                    for p in range(2):
                        for o in range(2):
                            own.forward(near, *v, *before, p, o)
            tiles.build(grid_ref, mics(pair, 0), turns, half, odd, pair, 0)
            total += tiles.adjoint((wc, ws), half, odd, pair, 0)
            if before is not None:
                tiles.forward(far, *v, *before, pair, 1)
            tiles.build(grid_ref, mics(pair, 1), turns, half, odd, pair, 1)
            return total

        total = pair_body(0, total, True)
        total = lax.fori_loop(1, 6, lambda pair, total: pair_body(pair, total, False), total)
        total += tiles.adjoint((wc, ws), half, odd, 5, 1)
        grad_ref[:, span(half * 2 + odd)] = total
        v = total.astype(BF16) * scale
        return v, swapped(v)

    v = one_step(0, 0, None, None)
    v = one_step(0, 1, v, (0, 0))
    v = one_step(1, 0, v, (0, 1))
    v = one_step(1, 1, v, (1, 0))
    for p in range(2):
        for o in range(2):
            own.forward(near, *v, 1, 1, p, o)

    def tail(pair, carry):
        tiles.forward(far, *v, 1, 1, pair, 0)
        tiles.forward(far, *v, 1, 1, pair, 1)
        return carry

    lax.fori_loop(0, 6, tail, 0)
    store_image(image_ref, near, 0)
    store_image(image_ref, far, 1)


def again_kernel(scale, q_ref, grad0_ref, *refs):
    own, tiles = Tiles(refs[:8]), Tiles(refs[8:16])
    packed_ref, image_ref, sums_ref, along_ref, wa, wb, wc, wd, near, far, grad_ref = refs[16:]
    for block in range(4):
        for chunk in range(4):
            real = jnp.concatenate([q_ref[4 * chunk + 2 * p, block] for p in range(2)], axis=1)
            imag = jnp.concatenate([q_ref[4 * chunk + 2 * p + 1, block] for p in range(2)], axis=1)
            if block == 0:
                set_weights(wa, wb, chunk, real, imag, scale)
            else:
                set_weights(wc, wd, (block - 1) * 4 + chunk, real, imag, scale)
    near[...] = jnp.zeros_like(near)
    far[...] = jnp.zeros_like(far)
    sums_ref[...] = jnp.zeros_like(sums_ref)

    def forward(v, half, odd):
        for o in range(2):
            for image, (c_ref, s_ref) in ((near, own.get(odd, o)), (far, tiles.get(odd, o))):
                image[o] += dot_nn(v[0], c_ref[span(half), :]) + dot_nn(v[1], s_ref[span(half), :])

    def adjoint(half, odd):
        total = None
        for o in range(2):
            for w_c, w_s, (c_ref, s_ref) in ((wa, wb, own.get(odd, o)), (wc, wd, tiles.get(odd, o))):
                value = dot_nt(w_c[o], c_ref[span(half), :]) + dot_nt(w_s[o], s_ref[span(half), :])
                total = value if total is None else total + value
        return total

    def finish(half, odd, total):
        cols = span(half * 2 + odd)
        g0 = grad0_ref[:, cols]
        grad_ref[:, cols] = total
        sums_ref[0:1] += lane_sums(g0 * g0)
        sums_ref[1:2] += lane_sums(g0 * total)
        sums_ref[2:3] += lane_sums(total * total)
        v = total.astype(BF16) * scale
        return v, swapped(v)

    v = finish(0, 0, adjoint(0, 0))
    for half, odd, before in ((0, 1, (0, 0)), (1, 0, (0, 1)), (1, 1, (1, 0))):
        total = adjoint(half, odd)
        forward(v, *before)
        v = finish(half, odd, total)
    forward(v, 1, 1)
    store_image(image_ref, near, 0)
    store_image(image_ref, far, 1)
    gg = jnp.sum(sums_ref[0:1], axis=1, keepdims=True)
    gh = jnp.sum(sums_ref[1:2], axis=1, keepdims=True)
    along = coefficient(gg, gh)
    along_ref[...] = jnp.broadcast_to(along, (8, 128))
    packed_ref[0:32] = grad0_ref[...].astype(BF16)
    packed_ref[32:64] = (grad_ref[...] - along * grad0_ref[...]).astype(BF16)


def coefficient(aa, ab):
    value = jnp.where(aa > 0.0, ab / jnp.where(aa > 0.0, aa, 1.0), 0.0)
    return value.astype(BF16).astype(F32)


def total_of(parts_ref):
    total = parts_ref[0].astype(F32)
    for j in range(1, 16):
        total += parts_ref[j].astype(F32)
    return total


def gather_kernel(parts_ref, shard_ref, copies_ref):
    total = total_of(parts_ref)
    shard_ref[...] = total
    low = total.astype(BF16)
    for j in range(16):
        copies_ref[j] = low


def pack_sums(sums, rest):
    high, middle, low = three(sums[:, 0:64] + sums[:, 64:128])
    left = jnp.concatenate([high, low], axis=0)
    right = jnp.concatenate([middle, jnp.zeros_like(low)], axis=0)
    return jnp.concatenate([jnp.concatenate([left, right], axis=1), rest], axis=0).astype(BF16)


def unpack_sums(tile):
    tile = tile.astype(F32)
    return tile[0:6] + jnp.concatenate([tile[6:12, 0:64], jnp.zeros((6, 64), F32)], axis=1), tile[12:16]


def spread_kernel(mic_ref, parts_ref, q_ref, sums_ref, along_ref, out_ref, shard):
    total = total_of(parts_ref)
    q = q_ref[...]

    def flat(x):
        return lane_sums(x.reshape(64, 128))

    near = sums_ref[0:3, 0:128] + sums_ref[0:3, 128:256]
    qq, qp = flat(q * q), flat(q * total)
    sums = jnp.concatenate([near, qq, qp, flat(total * total)], axis=0)
    along = coefficient(jnp.sum(qq, axis=1, keepdims=True), jnp.sum(qp, axis=1, keepdims=True))
    shard[...] = total - along * q
    rest = jnp.concatenate([jnp.broadcast_to(along, (1, 128)), along_ref[0:1], jnp.zeros((2, 128), F32)], axis=0)
    tile = pack_sums(sums, rest)
    for t in range(4):
        s = lax.rem(t + 4 - mic_ref[0], 4)
        a = q_ref[s]
        high = a.astype(BF16)
        middle = (a - high.astype(F32)).astype(BF16)
        off = shard[s].astype(BF16)
        for k in range(4):
            out_ref[t * 4 + k, 0:16] = high
            out_ref[t * 4 + k, 16:32] = middle
            out_ref[t * 4 + k, 32:48] = off
            out_ref[t * 4 + k, 48:64] = tile


def relay_kernel(bin_ref, recv_ref, out_ref, along_ref):
    sums = unpack_sums(recv_ref[0, 48:64])[0]
    for j in range(1, 16):
        sums += unpack_sums(recv_ref[j, 48:64])[0]
    rest = []
    for m in range(4):
        slot = m * 4 + bin_ref[0]
        piece = recv_ref[slot, 0:48]
        for j in range(16):
            out_ref[j, m * 48 : m * 48 + 48] = piece
        values = recv_ref[slot, 48:64].astype(F32)
        rest.append(values[12:13])
        along_ref[m : m + 1] = values[13:14]
    along_ref[4:8] = jnp.zeros((4, 128), F32)
    tile = pack_sums(sums, jnp.concatenate(rest, axis=0))
    for j in range(16):
        out_ref[j, 192:208] = tile


def last_kernel(mic_ref, recv_ref, along_ref, press_hbm, *refs):
    packs, (x_ref, r_ref, press_ref, sem) = refs[:4], refs[4:]
    copy = pltpu.make_async_copy(press_hbm, press_ref, sem)
    copy.start()
    total = unpack_sums(recv_ref[0, 192:208])[0]
    for j in range(1, 16):
        total += unpack_sums(recv_ref[j, 192:208])[0]
    total = jnp.sum(total, axis=1, keepdims=True)
    gg, gh, hh, qq, qp, pp = [total[i : i + 1] for i in range(6)]
    step0 = gg / qq
    norm1 = gg - 2.0 * step0 * gh + step0 * step0 * hh
    ratio = norm1 / gg
    image1 = (1.0 + ratio) * (1.0 + ratio) * qq - 2.0 * (1.0 + ratio) * step0 * qp + step0 * step0 * pp
    step1 = norm1 / image1
    lead = jnp.broadcast_to(step0 + step1 * (1.0 + ratio), (16, 128))
    tail = jnp.broadcast_to(step0 * step1, (16, 128))
    for s, pack in enumerate(packs):
        bin_at = lax.rem(mic_ref[0] + s, 4)
        first = lead - tail * along_ref[pl.ds(bin_at, 1)]
        for h in range(2):
            for c in range(8):
                cols = slice(c * 128, c * 128 + 128)
                g = pack[h * 16 : h * 16 + 16, cols].astype(F32)
                y = pack[32 + h * 16 : 48 + h * 16, cols].astype(F32)
                x_ref[bin_at, h, :, cols] = first * g - tail * y
    copy.wait()
    for h in range(2):
        for c in range(8):
            j, cols = 2 * c + h, slice(c * 128, c * 128 + 128)
            rest = unpack_sums(recv_ref[j, 192:208])[1]
            for m in range(4):
                q = recv_ref[j, m * 48 : m * 48 + 16].astype(F32) + recv_ref[j, m * 48 + 16 : m * 48 + 32].astype(F32)
                off = recv_ref[j, m * 48 + 32 : m * 48 + 48].astype(F32)
                r_ref[m, h, :, cols] = press_ref[m, h, :, cols] - (lead - tail * rest[m : m + 1]) * q + tail * off


def call(kernel, name, in_specs, out_shape, scratch=(), limit=4, work=0):
    return pl.pallas_call(
        kernel,
        in_specs=in_specs,
        out_specs=jax.tree.map(lambda _: VM, out_shape),
        out_shape=out_shape,
        scratch_shapes=list(scratch),
        compiler_params=pltpu.CompilerParams(vmem_limit_bytes=limit << 20),
        cost_estimate=pl.CostEstimate(flops=work, bytes_accessed=0, transcendentals=0) if work else None,
        name=name,
    )


def array(*shape, dtype=F32):
    return jax.ShapeDtypeStruct(shape, dtype)


def ahead(x, shift):
    return lax.ppermute(x, "mic", [((t + shift) % 4, t) for t in range(4)])


def body(grid_points, mic_coords, wavenumbers, pressures):
    scale = 1.0 / math.sqrt(grid_points.shape[1] * lax.axis_size("grid"))
    mic, bin_at = [jnp.reshape(lax.axis_index(name), (1,)).astype(jnp.int32) for name in ("mic", "bin")]
    flat = pressures.reshape(4, 32, 1024)

    points, turns, *packs = call(
        prepare_kernel,
        "prepare",
        [SM, HBM, HBM, HBM, HBM],
        [pltpu.VMEM((1024, 8), F32), pltpu.VMEM((8, 128), F32)] + [pltpu.VMEM((48, 1024), BF16)] * 4,
        [
            pltpu.SMEM((4,), F32),
            pltpu.VMEM((4, 32, 1024), F32),
            pltpu.VMEM((3, 1024), F32),
            pltpu.VMEM((8, 1024), F32),
            pltpu.SemaphoreType.DMA((4,)),
        ],
        limit=60,
    )(mic, wavenumbers, flat, mic_coords, grid_points)
    packs[1:] = [ahead(pack, s) for s, pack in zip((1, 2, 3), packs[1:])]

    def held(width):
        return [pltpu.VMEM((512, width), BF16)] * 8

    weights_near = [pltpu.VMEM((2, 32, 512), BF16)] * 2
    weights_far = [pltpu.VMEM((2, 32, 1536), BF16)] * 2
    images = [pltpu.VMEM((2, 32, 512), F32), pltpu.VMEM((2, 32, 1536), F32)]
    *near, head = call(
        functools.partial(own_kernel, scale),
        "own",
        [VM] * 3,
        held(512) + [array(32, 1024)],
        weights_near + [pltpu.VMEM((8, 1024), F32)],
    )(packs[0], turns, points)
    near = [pltpu.with_memory_space_constraint(t, pltpu.VMEM) for t in near]
    image_type = array(8, 2, 4, 16, 128, dtype=BF16)
    *far, grad0, part0 = call(
        functools.partial(rest_kernel, scale),
        "rest",
        [VM] * 14,
        held(1536) + [array(32, 1024), image_type],
        weights_far + images + [pltpu.VMEM((8, 3072), F32)],
    )(turns, points, *packs[1:], head, *near)
    far = [pltpu.with_memory_space_constraint(t, pltpu.VMEM) for t in far]

    parts = lax.all_to_all(part0.reshape(16, 4, 16, 128), "grid", 0, 0)
    image0, copies = call(
        gather_kernel, "gather", [VM], [array(4, 16, 128), array(16, 4, 16, 128, dtype=BF16)]
    )(parts)
    rounded = lax.all_to_all(copies, "grid", 0, 0)

    packed, part1, sums, along = call(
        functools.partial(again_kernel, scale),
        "again",
        [VM] * 18,
        [array(64, 1024, dtype=BF16), image_type, array(8, EDGE), array(8, 128)],
        weights_near + weights_far + images + [pltpu.VMEM((32, 1024), F32)],
        work=8 << 30,
    )(rounded, grad0, *near, *far)

    hops = [packed] + [ahead(packed, s) for s in (1, 2, 3)]
    parts = lax.all_to_all(part1.reshape(16, 4, 16, 128), "grid", 0, 0)
    sent = call(
        spread_kernel, "spread", [SM] + [VM] * 4, array(16, 64, 128, dtype=BF16), [pltpu.VMEM((4, 16, 128), F32)]
    )(mic, parts, image0, sums, along)
    recv = lax.all_to_all(sent, ("mic", "bin"), 0, 0)
    sent, alongs = call(relay_kernel, "relay", [SM, VM], [array(16, 208, 128, dtype=BF16), array(8, 128)])(bin_at, recv)
    recv = lax.all_to_all(sent, "grid", 0, 0)
    out_type = array(4, 2, 16, 1024)
    return call(
        last_kernel,
        "last",
        [SM, VM, VM, HBM] + [VM] * 4,
        [out_type, out_type],
        [pltpu.VMEM((4, 2, 16, 1024), F32), pltpu.SemaphoreType.DMA],
    )(mic, recv, alongs, pressures, *hops)


def solution(mesh):
    placed = (P(None, "grid"), P(None, "mic"), P("bin"), P("bin", None, None, "mic"))
    return jax.shard_map(
        body,
        mesh=mesh,
        in_specs=placed,
        out_specs=(P("bin", None, None, "grid"), P("bin", None, None, "mic")),
        check_vma=False,
    )
```

```python
import functools
import math

import jax
import jax.numpy as jnp
from jax import lax
from jax.experimental import pallas as pl
from jax.experimental.pallas import tpu as pltpu
from jax.sharding import PartitionSpec as P

F32, BF16 = jnp.float32, jnp.bfloat16
QUARTER = (2.641753911972046, -1.0863767862319946, 0.13400563597679138, -0.0077399080619215965)
SQUARE = 2.0 * math.sqrt(2.0)
ROOT = math.sqrt(2.0)
ROWS, LANES, EDGE = 16, 256, 256
VM = pl.BlockSpec(memory_space=pltpu.VMEM)
SM = pl.BlockSpec(memory_space=pltpu.SMEM)
ANY = pl.BlockSpec(memory_space=pl.ANY)
HBM = pl.BlockSpec(memory_space=pltpu.HBM)


def steering(gx, gy, gz, mx, my, mz, turns):
    dx, dy, dz = gx - mx, gy - my, gz - mz
    square = dx * dx + dy * dy + dz * dz
    inverse = lax.rsqrt(square)
    cycles = (square * inverse) * turns
    part = cycles - jnp.round(cycles)
    t = part * part
    s = QUARTER[3]
    for k in (2, 1, 0):
        s = s * t + QUARTER[k]
    s = s * part
    q = s * s
    w = SQUARE - q
    half_sin = s * (w * lax.rsqrt(w))
    half_cos = ROOT - q
    scaled = half_sin * inverse
    return (inverse - scaled * half_sin).astype(BF16), (scaled * half_cos).astype(BF16)


def dot_nt(a, b):
    return lax.dot_general(a, b, (((1,), (1,)), ((), ())), preferred_element_type=F32)


def dot_nn(a, b):
    return lax.dot_general(a, b, (((1,), (0,)), ((), ())), preferred_element_type=F32)


def multiple(x, m):
    return x if isinstance(x, int) else pl.multiple_of(x, m)


def span(index):
    return pl.ds(multiple(index * EDGE, EDGE), EDGE)


def lane_sums(x):
    return jnp.sum(x, axis=0, keepdims=True)


def swapped(v):
    return jnp.concatenate([v[16:32], -v[0:16]], axis=0)


class Tiles:
    def __init__(self, refs):
        self.refs = refs

    def get(self, step_odd, chunk_odd):
        at = (step_odd * 2 + chunk_odd) * 2
        return self.refs[at], self.refs[at + 1]

    def build(self, grid_ref, mics, turns, half, odd, pair, chunk_odd):
        c_ref, s_ref = self.get(odd, chunk_odd)
        for block in range(EDGE // ROWS):
            rows = pl.ds(multiple((half * 2 + odd) * EDGE + block * ROWS, ROWS), ROWS)
            g = [jnp.broadcast_to(grid_ref[rows, d : d + 1], (ROWS, LANES)) for d in range(3)]
            c, s = steering(*g, *mics, turns)
            at = (pl.ds(multiple(half * EDGE + block * ROWS, ROWS), ROWS), span(pair))
            c_ref[at] = c
            s_ref[at] = s

    def adjoint(self, weights, half, odd, pair, chunk_odd):
        c_ref, s_ref = self.get(odd, chunk_odd)
        wc, ws = weights[0], weights[1]
        at = (span(half), span(pair))
        cols = span(pair)
        return dot_nt(wc[chunk_odd, :, cols], c_ref[at]) + dot_nt(ws[chunk_odd, :, cols], s_ref[at])

    def forward(self, image, v, v2, half, odd, pair, chunk_odd):
        c_ref, s_ref = self.get(odd, chunk_odd)
        at = (span(half), span(pair))
        image[chunk_odd, :, span(pair)] += dot_nn(v, c_ref[at]) + dot_nn(v2, s_ref[at])


def three(x):
    high = x.astype(BF16).astype(F32)
    left = x - high
    middle = left.astype(BF16).astype(F32)
    return high, middle, (left - middle).astype(BF16).astype(F32)


def prepare_kernel(mic_ref, bin_ref, grid_ref, wave_hbm, press_hbm, coords_hbm, points_hbm, g_ref, turns_ref, p0, p1, p2, p3, press, *scratch):
    wave_ref, coords, pad, sems = scratch
    copies = [
        pltpu.make_async_copy(press_hbm, press, sems.at[0]),
        pltpu.make_async_copy(coords_hbm, coords, sems.at[1]),
        pltpu.make_async_copy(points_hbm, pad.at[0:3], sems.at[2]),
        pltpu.make_async_copy(wave_hbm, wave_ref, sems.at[3]),
    ]
    for copy in copies:
        copy.start()
    for copy in copies:
        copy.wait()
    turns_ref[...] = jnp.full((8, 128), wave_ref[mic_ref[0]] * (0.5 / math.pi), F32)
    high, middle, low = [part.astype(BF16) for part in three(coords[...])]
    for s, out in enumerate((p0, p1, p2, p3)):
        out[0:32] = press[lax.rem(mic_ref[0] + 4 - s, 4)].astype(BF16)
        out[32:35], out[35:38], out[38:41] = high, middle, low
        out[41:48] = jnp.zeros((7, 1024), BF16)
    pad[3:8] = jnp.zeros((5, 1024), F32)
    for r in range(8):
        g_ref[r * 128 : r * 128 + 128, :] = pad[:, r * 128 : r * 128 + 128].T


def whole_coords(pack):
    parts = pack[32:48].astype(F32)
    return (parts[0:3] + parts[3:6]) + parts[6:9]


def set_weights(wc, ws, chunk, real, imag, scale):
    odd, cols = chunk % 2, slice((chunk // 2) * EDGE, (chunk // 2) * EDGE + EDGE)
    real, imag = real * scale, imag * scale
    wc[odd, 0:16, cols] = real
    wc[odd, 16:32, cols] = imag
    ws[odd, 0:16, cols] = -imag
    ws[odd, 16:32, cols] = real


def own_kernel(scale, pack, turns_ref, grid_ref, *refs):
    tiles, grad_ref, wc, ws, coords = Tiles(refs[:8]), refs[8], refs[9], refs[10], refs[11]
    turns = turns_ref[0:1, 0:1]
    for chunk in range(4):
        w = pack[0:32, chunk * EDGE : chunk * EDGE + EDGE]
        set_weights(wc, ws, chunk, w[0:16], w[16:32], scale)
    coords[0:3] = whole_coords(pack)

    def mics(chunk):
        return [coords[d : d + 1, chunk * EDGE : chunk * EDGE + EDGE] for d in range(3)]

    def half_step(half, carry):
        late = None
        for odd in range(2):
            total = jnp.zeros((32, EDGE), F32)
            for pair in range(2):
                for chunk_odd in range(2):
                    if late is not None:
                        value = tiles.adjoint((wc, ws), half, *late)
                        if late[0] == odd:
                            total += value
                        else:
                            grad_ref[:, span(half * 2 + late[0])] = done + value
                    tiles.build(grid_ref, mics(pair * 2 + chunk_odd), turns, half, odd, pair, chunk_odd)
                    late = (odd, pair, chunk_odd)
            done = total
        grad_ref[:, span(half * 2 + 1)] = done + tiles.adjoint((wc, ws), half, *late)
        return carry

    lax.fori_loop(0, 2, half_step, 0)


def store_image(out_ref, image, first):
    for odd in range(2):
        for pair in range(image.shape[2] // EDGE):
            for piece in range(2):
                tile = (pair * 2 + odd) * 2 + piece
                s, c = tile // 8 + first, tile % 8
                lo = pair * EDGE + piece * 128
                for h in range(2):
                    out_ref[c, h, s] = image[odd, h * 16 : h * 16 + 16, lo : lo + 128].astype(BF16)


def rest_kernel(scale, turns_ref, grid_ref, p1, p2, p3, head_ref, *refs):
    own, tiles = Tiles(refs[:8]), Tiles(refs[8:16])
    grad_ref, image_ref, wc, ws, near, far, coords = refs[16:]
    turns = turns_ref[0:1, 0:1]
    for s, pack in enumerate((p1, p2, p3)):
        for chunk in range(4):
            w = pack[0:32, chunk * EDGE : chunk * EDGE + EDGE]
            set_weights(wc, ws, s * 4 + chunk, w[0:16], w[16:32], scale)
        coords[0:3, s * 1024 : s * 1024 + 1024] = whole_coords(pack)
    near[...] = jnp.zeros_like(near)
    far[...] = jnp.zeros_like(far)

    def mics(pair, chunk_odd):
        lo = pl.ds(multiple((pair * 2 + chunk_odd) * EDGE, EDGE), EDGE)
        return [coords[d : d + 1, lo] for d in range(3)]

    def one_step(half, odd, v, before):
        total = head_ref[:, span(half * 2 + odd)]

        def pair_body(pair, total, first):
            if not first:
                total += tiles.adjoint((wc, ws), half, odd, pair - 1, 1)
            if before is not None:
                tiles.forward(far, *v, *before, pair, 0)
                if first:
                    for p in range(2):
                        for o in range(2):
                            own.forward(near, *v, *before, p, o)
            tiles.build(grid_ref, mics(pair, 0), turns, half, odd, pair, 0)
            total += tiles.adjoint((wc, ws), half, odd, pair, 0)
            if before is not None:
                tiles.forward(far, *v, *before, pair, 1)
            tiles.build(grid_ref, mics(pair, 1), turns, half, odd, pair, 1)
            return total

        total = pair_body(0, total, True)
        total = lax.fori_loop(1, 6, lambda pair, total: pair_body(pair, total, False), total)
        total += tiles.adjoint((wc, ws), half, odd, 5, 1)
        grad_ref[:, span(half * 2 + odd)] = total
        v = total.astype(BF16) * scale
        return v, swapped(v)

    v = one_step(0, 0, None, None)
    v = one_step(0, 1, v, (0, 0))
    v = one_step(1, 0, v, (0, 1))
    v = one_step(1, 1, v, (1, 0))
    for p in range(2):
        for o in range(2):
            own.forward(near, *v, 1, 1, p, o)

    def tail(pair, carry):
        tiles.forward(far, *v, 1, 1, pair, 0)
        tiles.forward(far, *v, 1, 1, pair, 1)
        return carry

    lax.fori_loop(0, 6, tail, 0)
    store_image(image_ref, near, 0)
    store_image(image_ref, far, 1)


def again_kernel(scale, q_ref, grad0_ref, *refs):
    own, tiles = Tiles(refs[:8]), Tiles(refs[8:16])
    packed_ref, image_ref, sums_ref, along_ref, wa, wb, wc, wd, near, far, grad_ref = refs[16:]
    for block in range(4):
        for chunk in range(4):
            real = jnp.concatenate([q_ref[4 * chunk + 2 * p, block] for p in range(2)], axis=1)
            imag = jnp.concatenate([q_ref[4 * chunk + 2 * p + 1, block] for p in range(2)], axis=1)
            if block == 0:
                set_weights(wa, wb, chunk, real, imag, scale)
            else:
                set_weights(wc, wd, (block - 1) * 4 + chunk, real, imag, scale)
    near[...] = jnp.zeros_like(near)
    far[...] = jnp.zeros_like(far)
    sums_ref[...] = jnp.zeros_like(sums_ref)

    def forward(v, half, odd):
        for o in range(2):
            for image, (c_ref, s_ref) in ((near, own.get(odd, o)), (far, tiles.get(odd, o))):
                image[o] += dot_nn(v[0], c_ref[span(half), :]) + dot_nn(v[1], s_ref[span(half), :])

    def adjoint(half, odd):
        total = None
        for o in range(2):
            for w_c, w_s, (c_ref, s_ref) in ((wa, wb, own.get(odd, o)), (wc, wd, tiles.get(odd, o))):
                value = dot_nt(w_c[o], c_ref[span(half), :]) + dot_nt(w_s[o], s_ref[span(half), :])
                total = value if total is None else total + value
        return total

    def finish(half, odd, total):
        cols = span(half * 2 + odd)
        g0 = grad0_ref[:, cols]
        grad_ref[:, cols] = total
        sums_ref[0:1] += lane_sums(g0 * g0)
        sums_ref[1:2] += lane_sums(g0 * total)
        sums_ref[2:3] += lane_sums(total * total)
        v = total.astype(BF16) * scale
        return v, swapped(v)

    v = finish(0, 0, adjoint(0, 0))
    for half, odd, before in ((0, 1, (0, 0)), (1, 0, (0, 1)), (1, 1, (1, 0))):
        total = adjoint(half, odd)
        forward(v, *before)
        v = finish(half, odd, total)
    forward(v, 1, 1)
    store_image(image_ref, near, 0)
    store_image(image_ref, far, 1)
    gg = jnp.sum(sums_ref[0:1], axis=1, keepdims=True)
    gh = jnp.sum(sums_ref[1:2], axis=1, keepdims=True)
    along = coefficient(gg, gh)
    along_ref[...] = jnp.broadcast_to(along, (8, 128))
    packed_ref[0:32] = grad0_ref[...].astype(BF16)
    packed_ref[32:64] = (grad_ref[...] - along * grad0_ref[...]).astype(BF16)


def coefficient(aa, ab):
    value = jnp.where(aa > 0.0, ab / jnp.where(aa > 0.0, aa, 1.0), 0.0)
    return value.astype(BF16).astype(F32)


def total_of(parts_ref):
    total = parts_ref[0].astype(F32)
    for j in range(1, 16):
        total += parts_ref[j].astype(F32)
    return total


def gather_kernel(parts_ref, shard_ref, copies_ref):
    total = total_of(parts_ref)
    shard_ref[...] = total
    low = total.astype(BF16)
    for j in range(16):
        copies_ref[j] = low


def pack_sums(sums, rest):
    high, middle, low = three(sums[:, 0:64] + sums[:, 64:128])
    left = jnp.concatenate([high, low], axis=0)
    right = jnp.concatenate([middle, jnp.zeros_like(low)], axis=0)
    return jnp.concatenate([jnp.concatenate([left, right], axis=1), rest], axis=0).astype(BF16)


def unpack_sums(tile):
    tile = tile.astype(F32)
    return tile[0:6] + jnp.concatenate([tile[6:12, 0:64], jnp.zeros((6, 64), F32)], axis=1), tile[12:16]


def spread_kernel(mic_ref, grid_ref, parts_ref, q_ref, sums_ref, along_ref, p0, p1, p2, p3, out_ref, off_press, off_image):
    total = total_of(parts_ref)
    q = q_ref[...]
    rows = pl.ds(pl.multiple_of(lax.rem(grid_ref[0], 2) * 16, 16), 16)
    cols = pl.ds(pl.multiple_of(lax.div(grid_ref[0], 2) * 128, 128), 128)
    press = jnp.stack([pack[rows, cols] for pack in (p0, p1, p2, p3)]).astype(F32)

    def flat(x):
        return lane_sums(x.reshape(64, 128))

    def part_along(aa, ab):
        return coefficient(jnp.sum(aa, axis=1, keepdims=True), jnp.sum(ab, axis=1, keepdims=True))

    near = sums_ref[0:3, 0:128] + sums_ref[0:3, 128:256]
    qq, qp = flat(q * q), flat(q * total)
    sums = jnp.concatenate([near, qq, qp, flat(total * total)], axis=0)
    on_press = part_along(flat(press * press), flat(press * q))
    on_image = part_along(qq, qp)
    off_press[...] = q - on_press * press
    off_image[...] = total - on_image * q
    both = jnp.concatenate([jnp.broadcast_to(on_image, (1, 64)), jnp.broadcast_to(on_press, (1, 64))], axis=1)
    tile = pack_sums(sums, jnp.concatenate([both, along_ref[0:1], jnp.zeros((2, 128), F32)], axis=0))
    for t in range(4):
        s = lax.rem(t + 4 - mic_ref[0], 4)
        first, second = off_press[s].astype(BF16), off_image[s].astype(BF16)
        for k in range(4):
            out_ref[t * 4 + k, 0:16] = first
            out_ref[t * 4 + k, 16:32] = second
            out_ref[t * 4 + k, 32:48] = tile


def relay_kernel(bin_ref, recv_ref, out_ref, along_ref):
    sums = unpack_sums(recv_ref[0, 32:48])[0]
    for j in range(1, 16):
        sums += unpack_sums(recv_ref[j, 32:48])[0]
    rest = []
    for m in range(4):
        slot = m * 4 + bin_ref[0]
        piece = recv_ref[slot, 0:32]
        for j in range(16):
            out_ref[j, m * 32 : m * 32 + 32] = piece
        values = recv_ref[slot, 32:48].astype(F32)
        rest.append(values[12:13])
        along_ref[m : m + 1] = values[13:14]
    along_ref[4:8] = jnp.zeros((4, 128), F32)
    tile = pack_sums(sums, jnp.concatenate(rest, axis=0))
    for j in range(16):
        out_ref[j, 128:144] = tile


def last_kernel(mic_ref, recv_ref, along_ref, press_ref, *refs):
    packs, (x_ref, r_ref) = refs[:4], refs[4:]
    total = unpack_sums(recv_ref[0, 128:144])[0]
    for j in range(1, 16):
        total += unpack_sums(recv_ref[j, 128:144])[0]
    total = jnp.sum(total, axis=1, keepdims=True)
    gg, gh, hh, qq, qp, pp = [total[i : i + 1] for i in range(6)]
    step0 = gg / qq
    norm1 = gg - 2.0 * step0 * gh + step0 * step0 * hh
    ratio = norm1 / gg
    image1 = (1.0 + ratio) * (1.0 + ratio) * qq - 2.0 * (1.0 + ratio) * step0 * qp + step0 * step0 * pp
    step1 = norm1 / image1
    lead = jnp.broadcast_to(step0 + step1 * (1.0 + ratio), (16, 128))
    tail = jnp.broadcast_to(step0 * step1, (16, 128))
    for s, pack in enumerate(packs):
        bin_at = lax.rem(mic_ref[0] + s, 4)
        first = lead - tail * along_ref[pl.ds(bin_at, 1)]
        for h in range(2):
            for c in range(8):
                cols = slice(c * 128, c * 128 + 128)
                g = pack[h * 16 : h * 16 + 16, cols].astype(F32)
                y = pack[32 + h * 16 : 48 + h * 16, cols].astype(F32)
                x_ref[bin_at, h, :, cols] = first * g - tail * y
    for h in range(2):
        for c in range(8):
            j, cols = 2 * c + h, slice(c * 128, c * 128 + 128)
            rest = unpack_sums(recv_ref[j, 128:144])[1]
            for m in range(4):
                press = press_ref[m, h * 16 : h * 16 + 16, cols]
                q = recv_ref[j, m * 32 : m * 32 + 16].astype(F32)
                q += rest[m : m + 1, 64:65] * press.astype(BF16).astype(F32)
                off = recv_ref[j, m * 32 + 16 : m * 32 + 32].astype(F32)
                r_ref[m, h, :, cols] = press - (lead - tail * rest[m : m + 1, 0:1]) * q + tail * off


def call(kernel, name, in_specs, out_shape, scratch=(), limit=4, work=0):
    return pl.pallas_call(
        kernel,
        in_specs=in_specs,
        out_specs=jax.tree.map(lambda _: VM, out_shape),
        out_shape=out_shape,
        scratch_shapes=list(scratch),
        compiler_params=pltpu.CompilerParams(vmem_limit_bytes=limit << 20),
        cost_estimate=pl.CostEstimate(flops=work, bytes_accessed=0, transcendentals=0) if work else None,
        name=name,
    )


def array(*shape, dtype=F32):
    return jax.ShapeDtypeStruct(shape, dtype)


def ahead(x, shift):
    return lax.ppermute(x, "mic", [((t + shift) % 4, t) for t in range(4)])


def body(grid_points, mic_coords, wavenumbers, pressures):
    scale = 1.0 / math.sqrt(grid_points.shape[1] * lax.axis_size("grid"))
    mic, bin_at, grid_at = [jnp.reshape(lax.axis_index(name), (1,)).astype(jnp.int32) for name in ("mic", "bin", "grid")]
    flat = pressures.reshape(4, 32, 1024)

    points, turns, *packs, press = call(
        prepare_kernel,
        "prepare",
        [SM, SM, SM, HBM, HBM, HBM, HBM],
        [pltpu.VMEM((1024, 8), F32), pltpu.VMEM((8, 128), F32)] + [pltpu.VMEM((48, 1024), BF16)] * 4
        + [pltpu.VMEM((4, 32, 1024), F32)],
        [
            pltpu.SMEM((4,), F32),
            pltpu.VMEM((3, 1024), F32),
            pltpu.VMEM((8, 1024), F32),
            pltpu.SemaphoreType.DMA((4,)),
        ],
        limit=60,
    )(mic, bin_at, grid_at, wavenumbers, flat, mic_coords, grid_points)
    packs[1:] = [ahead(pack, s) for s, pack in zip((1, 2, 3), packs[1:])]

    def held(width):
        return [pltpu.VMEM((512, width), BF16)] * 8

    weights_near = [pltpu.VMEM((2, 32, 512), BF16)] * 2
    weights_far = [pltpu.VMEM((2, 32, 1536), BF16)] * 2
    images = [pltpu.VMEM((2, 32, 512), F32), pltpu.VMEM((2, 32, 1536), F32)]
    *near, head = call(
        functools.partial(own_kernel, scale),
        "own",
        [VM] * 3,
        held(512) + [array(32, 1024)],
        weights_near + [pltpu.VMEM((8, 1024), F32)],
    )(packs[0], turns, points)
    near = [pltpu.with_memory_space_constraint(t, pltpu.VMEM) for t in near]
    image_type = array(8, 2, 4, 16, 128, dtype=BF16)
    *far, grad0, part0 = call(
        functools.partial(rest_kernel, scale),
        "rest",
        [VM] * 14,
        held(1536) + [array(32, 1024), image_type],
        weights_far + images + [pltpu.VMEM((8, 3072), F32)],
    )(turns, points, *packs[1:], head, *near)
    far = [pltpu.with_memory_space_constraint(t, pltpu.VMEM) for t in far]

    parts = lax.all_to_all(part0.reshape(16, 4, 16, 128), "grid", 0, 0)
    image0, copies = call(
        gather_kernel, "gather", [VM], [array(4, 16, 128), array(16, 4, 16, 128, dtype=BF16)]
    )(parts)
    rounded = lax.all_to_all(copies, "grid", 0, 0)

    packed, part1, sums, along = call(
        functools.partial(again_kernel, scale),
        "again",
        [VM] * 18,
        [array(64, 1024, dtype=BF16), image_type, array(8, EDGE), array(8, 128)],
        weights_near + weights_far + images + [pltpu.VMEM((32, 1024), F32)],
        work=8 << 30,
    )(rounded, grad0, *near, *far)

    near_hop = ahead(packed, 1)
    hops = [packed, near_hop, ahead(near_hop, 1), ahead(packed, 3)]
    parts = lax.all_to_all(part1.reshape(16, 4, 16, 128), "grid", 0, 0)
    sent = call(
        spread_kernel,
        "spread",
        [SM, SM] + [VM] * 8,
        array(16, 48, 128, dtype=BF16),
        [pltpu.VMEM((4, 16, 128), F32)] * 2,
    )(mic, grid_at, parts, image0, sums, along, *packs)
    recv = lax.all_to_all(sent, ("mic", "bin"), 0, 0)
    sent, alongs = call(relay_kernel, "relay", [SM, VM], [array(16, 144, 128, dtype=BF16), array(8, 128)])(bin_at, recv)
    recv = lax.all_to_all(sent, "grid", 0, 0)
    out_type = array(4, 2, 16, 1024)
    return call(
        last_kernel,
        "last",
        [SM] + [VM] * 7,
        [out_type, out_type],
    )(mic, recv, alongs, press, *hops)


def solution(mesh):
    placed = (P(None, "grid"), P(None, "mic"), P("bin"), P("bin", None, None, "mic"))
    return jax.shard_map(
        body,
        mesh=mesh,
        in_specs=placed,
        out_specs=(P("bin", None, None, "grid"), P("bin", None, None, "mic")),
        check_vma=False,
    )
```

```python
import functools
import math

import jax
import jax.numpy as jnp
from jax import lax
from jax.experimental import pallas as pl
from jax.experimental.pallas import tpu as pltpu
from jax.sharding import PartitionSpec as P

F32, BF16 = jnp.float32, jnp.bfloat16
QUARTER = (2.641753911972046, -1.0863767862319946, 0.13400563597679138, -0.0077399080619215965)
SQUARE = 2.0 * math.sqrt(2.0)
ROOT = math.sqrt(2.0)
ROWS, LANES, EDGE = 16, 256, 256
VM = pl.BlockSpec(memory_space=pltpu.VMEM)
SM = pl.BlockSpec(memory_space=pltpu.SMEM)
ANY = pl.BlockSpec(memory_space=pl.ANY)
HBM = pl.BlockSpec(memory_space=pltpu.HBM)


def steering(gx, gy, gz, mx, my, mz, turns):
    dx, dy, dz = gx - mx, gy - my, gz - mz
    square = dx * dx + dy * dy + dz * dz
    inverse = lax.rsqrt(square)
    cycles = (square * inverse) * turns
    part = cycles - jnp.round(cycles)
    t = part * part
    s = QUARTER[3]
    for k in (2, 1, 0):
        s = s * t + QUARTER[k]
    s = s * part
    q = s * s
    w = SQUARE - q
    half_sin = s * (w * lax.rsqrt(w))
    half_cos = ROOT - q
    scaled = half_sin * inverse
    return (inverse - scaled * half_sin).astype(BF16), (scaled * half_cos).astype(BF16)


def dot_nt(a, b):
    return lax.dot_general(a, b, (((1,), (1,)), ((), ())), preferred_element_type=F32)


def dot_nn(a, b):
    return lax.dot_general(a, b, (((1,), (0,)), ((), ())), preferred_element_type=F32)


def multiple(x, m):
    return x if isinstance(x, int) else pl.multiple_of(x, m)


def span(index):
    return pl.ds(multiple(index * EDGE, EDGE), EDGE)


def lane_sums(x):
    return jnp.sum(x, axis=0, keepdims=True)


def swapped(v):
    return jnp.concatenate([v[16:32], -v[0:16]], axis=0)


class Tiles:
    def __init__(self, refs):
        self.refs = refs

    def get(self, step_odd, chunk_odd):
        at = (step_odd * 2 + chunk_odd) * 2
        return self.refs[at], self.refs[at + 1]

    def build(self, grid_ref, mics, turns, half, odd, pair, chunk_odd):
        c_ref, s_ref = self.get(odd, chunk_odd)
        for block in range(EDGE // ROWS):
            rows = pl.ds(multiple((half * 2 + odd) * EDGE + block * ROWS, ROWS), ROWS)
            g = [jnp.broadcast_to(grid_ref[rows, d : d + 1], (ROWS, LANES)) for d in range(3)]
            c, s = steering(*g, *mics, turns)
            at = (pl.ds(multiple(half * EDGE + block * ROWS, ROWS), ROWS), span(pair))
            c_ref[at] = c
            s_ref[at] = s

    def adjoint(self, weights, half, odd, pair, chunk_odd):
        c_ref, s_ref = self.get(odd, chunk_odd)
        wc, ws = weights[0], weights[1]
        at = (span(half), span(pair))
        cols = span(pair)
        return dot_nt(wc[chunk_odd, :, cols], c_ref[at]) + dot_nt(ws[chunk_odd, :, cols], s_ref[at])

    def forward(self, image, v, v2, half, odd, pair, chunk_odd):
        c_ref, s_ref = self.get(odd, chunk_odd)
        at = (span(half), span(pair))
        image[chunk_odd, :, span(pair)] += dot_nn(v, c_ref[at]) + dot_nn(v2, s_ref[at])


def three(x):
    high = x.astype(BF16).astype(F32)
    left = x - high
    middle = left.astype(BF16).astype(F32)
    return high, middle, (left - middle).astype(BF16).astype(F32)


def prepare_kernel(mic_ref, bin_ref, grid_ref, wave_hbm, press_hbm, coords_hbm, points_hbm, g_ref, turns_ref, p0, p1, p2, p3, press, *scratch):
    wave_ref, coords, pad, sems = scratch
    copies = [
        pltpu.make_async_copy(press_hbm, press, sems.at[0]),
        pltpu.make_async_copy(coords_hbm, coords, sems.at[1]),
        pltpu.make_async_copy(points_hbm, pad.at[0:3], sems.at[2]),
        pltpu.make_async_copy(wave_hbm, wave_ref, sems.at[3]),
    ]
    for copy in copies:
        copy.start()
    for copy in copies:
        copy.wait()
    turns_ref[...] = jnp.full((8, 128), wave_ref[mic_ref[0]] * (0.5 / math.pi), F32)
    high, middle, low = [part.astype(BF16) for part in three(coords[...])]
    for s, out in enumerate((p0, p1, p2, p3)):
        out[0:32] = press[lax.rem(mic_ref[0] + 4 - s, 4)].astype(BF16)
        out[32:35], out[35:38], out[38:41] = high, middle, low
        out[41:48] = jnp.zeros((7, 1024), BF16)
    pad[3:8] = jnp.zeros((5, 1024), F32)
    for r in range(8):
        g_ref[r * 128 : r * 128 + 128, :] = pad[:, r * 128 : r * 128 + 128].T


def whole_coords(pack):
    parts = pack[32:48].astype(F32)
    return (parts[0:3] + parts[3:6]) + parts[6:9]


def set_weights(wc, ws, chunk, real, imag, scale):
    odd, cols = chunk % 2, slice((chunk // 2) * EDGE, (chunk // 2) * EDGE + EDGE)
    real, imag = real * scale, imag * scale
    wc[odd, 0:16, cols] = real
    wc[odd, 16:32, cols] = imag
    ws[odd, 0:16, cols] = -imag
    ws[odd, 16:32, cols] = real


def head_kernel(scale, count, turns_ref, grid_ref, *refs):
    packs, refs = refs[:count], refs[count:]
    if count > 1:
        before, refs = refs[0], refs[1:]
    tiles, (grad_ref, wc, ws, coords) = Tiles(refs[:8]), refs[8:]
    turns = turns_ref[0:1, 0:1]
    for s, pack in enumerate(packs):
        for chunk in range(4):
            w = pack[0:32, chunk * EDGE : chunk * EDGE + EDGE]
            set_weights(wc, ws, s * 4 + chunk, w[0:16], w[16:32], scale)
        coords[0:3, s * 1024 : s * 1024 + 1024] = whole_coords(pack)

    def mics(chunk):
        return [coords[d : d + 1, chunk * EDGE : chunk * EDGE + EDGE] for d in range(3)]

    def half_step(half, carry):
        late = done = None
        for odd in range(2):
            total = jnp.zeros((32, EDGE), F32) if count == 1 else before[:, span(half * 2 + odd)]
            for pair in range(2 * count):
                for chunk_odd in range(2):
                    if late is not None:
                        value = tiles.adjoint((wc, ws), half, *late)
                        if late[0] == odd:
                            total += value
                        else:
                            grad_ref[:, span(half * 2 + late[0])] = done + value
                    tiles.build(grid_ref, mics(pair * 2 + chunk_odd), turns, half, odd, pair, chunk_odd)
                    late = (odd, pair, chunk_odd)
            done = total
        grad_ref[:, span(half * 2 + 1)] = done + tiles.adjoint((wc, ws), half, *late)
        return carry

    lax.fori_loop(0, 2, half_step, 0)


def store_image(out_ref, image, blocks):
    for odd in range(2):
        for pair in range(image.shape[2] // EDGE):
            for piece in range(2):
                tile = (pair * 2 + odd) * 2 + piece
                s, c = blocks[tile // 8], tile % 8
                lo = pair * EDGE + piece * 128
                for h in range(2):
                    out_ref[c, h, s] = image[odd, h * 16 : h * 16 + 16, lo : lo + 128].astype(BF16)


BLOCKS = ((0,), (1, 3), (2,))


def rest_kernel(scale, turns_ref, grid_ref, pack, before, *refs):
    near, middle, tiles = Tiles(refs[:8]), Tiles(refs[8:16]), Tiles(refs[16:24])
    grad_ref, image_ref, wc, ws, coords = refs[24:29]
    images = refs[29:]
    turns = turns_ref[0:1, 0:1]
    for chunk in range(4):
        w = pack[0:32, chunk * EDGE : chunk * EDGE + EDGE]
        set_weights(wc, ws, chunk, w[0:16], w[16:32], scale)
    coords[0:3] = whole_coords(pack)
    for image in images:
        image[...] = jnp.zeros_like(image)
    tasks = []
    for group, image, blocks in zip((near, middle, tiles), images, BLOCKS):
        tasks += [(group, image, pair, odd) for pair in range(2 * len(blocks)) for odd in range(2)]

    def forward(some, v, half, odd):
        for group, image, pair, chunk_odd in some:
            group.forward(image, *v, half, odd, pair, chunk_odd)

    v = last = None
    for half, odd in ((0, 0), (0, 1), (1, 0), (1, 1)):
        total = before[:, span(half * 2 + odd)]
        for n in range(4):
            if n:
                total += tiles.adjoint((wc, ws), half, odd, *divmod(n - 1, 2))
            if last is not None:
                forward(tasks[4 * n : 4 * n + 4], v, *last)
            cols = slice(n * EDGE, n * EDGE + EDGE)
            tiles.build(grid_ref, [coords[d : d + 1, cols] for d in range(3)], turns, half, odd, *divmod(n, 2))
        total += tiles.adjoint((wc, ws), half, odd, 1, 1)
        grad_ref[:, span(half * 2 + odd)] = total
        v = total.astype(BF16) * scale
        v, last = (v, swapped(v)), (half, odd)
    forward(tasks, v, *last)
    for image, blocks in zip(images, BLOCKS):
        store_image(image_ref, image, blocks)


def again_kernel(scale, q_ref, grad0_ref, *refs):
    groups = Tiles(refs[:8]), Tiles(refs[8:16]), Tiles(refs[16:24])
    packed_ref, image_ref, sums_ref, along_ref, *refs = refs[24:]
    weights, images, grad_ref = (refs[0:2], refs[2:4], refs[4:6]), refs[6:9], refs[9]
    for pair, blocks in zip(weights, BLOCKS):
        for at, block in enumerate(blocks):
            for chunk in range(4):
                real = jnp.concatenate([q_ref[4 * chunk + 2 * p, block] for p in range(2)], axis=1)
                imag = jnp.concatenate([q_ref[4 * chunk + 2 * p + 1, block] for p in range(2)], axis=1)
                set_weights(*pair, at * 4 + chunk, real, imag, scale)
    for image in images:
        image[...] = jnp.zeros_like(image)
    sums_ref[...] = jnp.zeros_like(sums_ref)

    def forward(v, half, odd):
        for o in range(2):
            for image, group in zip(images, groups):
                c_ref, s_ref = group.get(odd, o)
                image[o] += dot_nn(v[0], c_ref[span(half), :]) + dot_nn(v[1], s_ref[span(half), :])

    def adjoint(half, odd):
        total = None
        for o in range(2):
            for (w_c, w_s), group in zip(weights, groups):
                c_ref, s_ref = group.get(odd, o)
                value = dot_nt(w_c[o], c_ref[span(half), :]) + dot_nt(w_s[o], s_ref[span(half), :])
                total = value if total is None else total + value
        return total

    def finish(half, odd, total):
        cols = span(half * 2 + odd)
        g0 = grad0_ref[:, cols]
        grad_ref[:, cols] = total
        sums_ref[0:1] += lane_sums(g0 * g0)
        sums_ref[1:2] += lane_sums(g0 * total)
        sums_ref[2:3] += lane_sums(total * total)
        v = total.astype(BF16) * scale
        return v, swapped(v)

    v = finish(0, 0, adjoint(0, 0))
    for half, odd, before in ((0, 1, (0, 0)), (1, 0, (0, 1)), (1, 1, (1, 0))):
        total = adjoint(half, odd)
        forward(v, *before)
        v = finish(half, odd, total)
    forward(v, 1, 1)
    for image, blocks in zip(images, BLOCKS):
        store_image(image_ref, image, blocks)
    gg = jnp.sum(sums_ref[0:1], axis=1, keepdims=True)
    gh = jnp.sum(sums_ref[1:2], axis=1, keepdims=True)
    along = coefficient(gg, gh)
    along_ref[...] = jnp.broadcast_to(along, (8, 128))
    packed_ref[0:32] = grad0_ref[...].astype(BF16)
    packed_ref[32:64] = (grad_ref[...] - along * grad0_ref[...]).astype(BF16)


def coefficient(aa, ab):
    value = jnp.where(aa > 0.0, ab / jnp.where(aa > 0.0, aa, 1.0), 0.0)
    return value.astype(BF16).astype(F32)


def total_of(parts_ref):
    total = parts_ref[0].astype(F32)
    for j in range(1, 16):
        total += parts_ref[j].astype(F32)
    return total


def gather_kernel(parts_ref, shard_ref, copies_ref):
    total = total_of(parts_ref)
    shard_ref[...] = total
    low = total.astype(BF16)
    for j in range(16):
        copies_ref[j] = low


def pack_sums(sums, rest):
    high, middle, low = three(sums[:, 0:64] + sums[:, 64:128])
    left = jnp.concatenate([high, low], axis=0)
    right = jnp.concatenate([middle, jnp.zeros_like(low)], axis=0)
    return jnp.concatenate([jnp.concatenate([left, right], axis=1), rest], axis=0).astype(BF16)


def unpack_sums(tile):
    tile = tile.astype(F32)
    return tile[0:6] + jnp.concatenate([tile[6:12, 0:64], jnp.zeros((6, 64), F32)], axis=1), tile[12:16]


def spread_kernel(mic_ref, grid_ref, parts_ref, q_ref, sums_ref, along_ref, p0, p1, p2, p3, out_ref, off_press, off_image):
    total = total_of(parts_ref)
    q = q_ref[...]
    rows = pl.ds(pl.multiple_of(lax.rem(grid_ref[0], 2) * 16, 16), 16)
    cols = pl.ds(pl.multiple_of(lax.div(grid_ref[0], 2) * 128, 128), 128)
    press = jnp.stack([pack[rows, cols] for pack in (p0, p1, p2, p3)]).astype(F32)

    def flat(x):
        return lane_sums(x.reshape(64, 128))

    def part_along(aa, ab):
        return coefficient(jnp.sum(aa, axis=1, keepdims=True), jnp.sum(ab, axis=1, keepdims=True))

    near = sums_ref[0:3, 0:128] + sums_ref[0:3, 128:256]
    qq, qp = flat(q * q), flat(q * total)
    sums = jnp.concatenate([near, qq, qp, flat(total * total)], axis=0)
    on_press = part_along(flat(press * press), flat(press * q))
    on_image = part_along(qq, qp)
    off_press[...] = q - on_press * press
    off_image[...] = total - on_image * q
    both = jnp.concatenate([jnp.broadcast_to(on_image, (1, 64)), jnp.broadcast_to(on_press, (1, 64))], axis=1)
    tile = pack_sums(sums, jnp.concatenate([both, along_ref[0:1], jnp.zeros((2, 128), F32)], axis=0))
    for t in range(4):
        s = lax.rem(t + 4 - mic_ref[0], 4)
        first, second = off_press[s].astype(BF16), off_image[s].astype(BF16)
        for k in range(4):
            out_ref[t * 4 + k, 0:16] = first
            out_ref[t * 4 + k, 16:32] = second
            out_ref[t * 4 + k, 32:48] = tile


def relay_kernel(bin_ref, recv_ref, out_ref, along_ref):
    sums = unpack_sums(recv_ref[0, 32:48])[0]
    for j in range(1, 16):
        sums += unpack_sums(recv_ref[j, 32:48])[0]
    rest = []
    for m in range(4):
        slot = m * 4 + bin_ref[0]
        piece = recv_ref[slot, 0:32]
        for j in range(16):
            out_ref[j, m * 32 : m * 32 + 32] = piece
        values = recv_ref[slot, 32:48].astype(F32)
        rest.append(values[12:13])
        along_ref[m : m + 1] = values[13:14]
    along_ref[4:8] = jnp.zeros((4, 128), F32)
    tile = pack_sums(sums, jnp.concatenate(rest, axis=0))
    for j in range(16):
        out_ref[j, 128:144] = tile


def last_kernel(mic_ref, recv_ref, along_ref, press_ref, *refs):
    packs, (x_ref, r_ref) = refs[:4], refs[4:]
    total = unpack_sums(recv_ref[0, 128:144])[0]
    for j in range(1, 16):
        total += unpack_sums(recv_ref[j, 128:144])[0]
    total = jnp.sum(total, axis=1, keepdims=True)
    gg, gh, hh, qq, qp, pp = [total[i : i + 1] for i in range(6)]
    step0 = gg / qq
    norm1 = gg - 2.0 * step0 * gh + step0 * step0 * hh
    ratio = norm1 / gg
    image1 = (1.0 + ratio) * (1.0 + ratio) * qq - 2.0 * (1.0 + ratio) * step0 * qp + step0 * step0 * pp
    step1 = norm1 / image1
    lead = jnp.broadcast_to(step0 + step1 * (1.0 + ratio), (16, 128))
    tail = jnp.broadcast_to(step0 * step1, (16, 128))
    for s, pack in enumerate(packs):
        bin_at = lax.rem(mic_ref[0] + s, 4)
        first = lead - tail * along_ref[pl.ds(bin_at, 1)]
        for h in range(2):
            for c in range(8):
                cols = slice(c * 128, c * 128 + 128)
                g = pack[h * 16 : h * 16 + 16, cols].astype(F32)
                y = pack[32 + h * 16 : 48 + h * 16, cols].astype(F32)
                x_ref[bin_at, h, :, cols] = first * g - tail * y
    for h in range(2):
        for c in range(8):
            j, cols = 2 * c + h, slice(c * 128, c * 128 + 128)
            rest = unpack_sums(recv_ref[j, 128:144])[1]
            for m in range(4):
                press = press_ref[m, h * 16 : h * 16 + 16, cols]
                q = recv_ref[j, m * 32 : m * 32 + 16].astype(F32)
                q += rest[m : m + 1, 64:65] * press.astype(BF16).astype(F32)
                off = recv_ref[j, m * 32 + 16 : m * 32 + 32].astype(F32)
                r_ref[m, h, :, cols] = press - (lead - tail * rest[m : m + 1, 0:1]) * q + tail * off


def call(kernel, name, in_specs, out_shape, scratch=(), limit=4, work=0):
    return pl.pallas_call(
        kernel,
        in_specs=in_specs,
        out_specs=jax.tree.map(lambda _: VM, out_shape),
        out_shape=out_shape,
        scratch_shapes=list(scratch),
        compiler_params=pltpu.CompilerParams(vmem_limit_bytes=limit << 20),
        cost_estimate=pl.CostEstimate(flops=work, bytes_accessed=0, transcendentals=0) if work else None,
        name=name,
    )


def array(*shape, dtype=F32):
    return jax.ShapeDtypeStruct(shape, dtype)


def ahead(x, shift):
    return lax.ppermute(x, "mic", [((t + shift) % 4, t) for t in range(4)])


def body(grid_points, mic_coords, wavenumbers, pressures):
    scale = 1.0 / math.sqrt(grid_points.shape[1] * lax.axis_size("grid"))
    mic, bin_at, grid_at = [jnp.reshape(lax.axis_index(name), (1,)).astype(jnp.int32) for name in ("mic", "bin", "grid")]
    flat = pressures.reshape(4, 32, 1024)

    points, turns, *packs, press = call(
        prepare_kernel,
        "prepare",
        [SM, SM, SM, HBM, HBM, HBM, HBM],
        [pltpu.VMEM((1024, 8), F32), pltpu.VMEM((8, 128), F32)] + [pltpu.VMEM((48, 1024), BF16)] * 4
        + [pltpu.VMEM((4, 32, 1024), F32)],
        [
            pltpu.SMEM((4,), F32),
            pltpu.VMEM((3, 1024), F32),
            pltpu.VMEM((8, 1024), F32),
            pltpu.SemaphoreType.DMA((4,)),
        ],
        limit=60,
    )(mic, bin_at, grid_at, wavenumbers, flat, mic_coords, grid_points)
    packs[1:] = [ahead(pack, s) for s, pack in zip((1, 2, 3), packs[1:])]

    def held(width):
        return [pltpu.VMEM((512, width), BF16)] * 8

    def weights(count):
        return [pltpu.VMEM((2, 32, 512 * count), BF16)] * 2

    def coords(count):
        return [pltpu.VMEM((8, 1024 * count), F32)]

    images = [pltpu.VMEM((2, 32, 512 * len(blocks)), F32) for blocks in BLOCKS]
    image_type = array(8, 2, 4, 16, 128, dtype=BF16)

    def stay(tiles):
        return [pltpu.with_memory_space_constraint(t, pltpu.VMEM) for t in tiles]

    *near, head = call(
        functools.partial(head_kernel, scale, 1),
        "own",
        [VM] * 3,
        held(512) + [array(32, 1024)],
        weights(1) + coords(1),
    )(turns, points, packs[0])
    near = stay(near)
    *middle, head = call(
        functools.partial(head_kernel, scale, 2),
        "middle",
        [VM] * 5,
        held(1024) + [array(32, 1024)],
        weights(2) + coords(2),
    )(turns, points, packs[1], packs[3], head)
    middle = stay(middle)
    *far, grad0, part0 = call(
        functools.partial(rest_kernel, scale),
        "rest",
        [VM] * 20,
        held(512) + [array(32, 1024), image_type],
        weights(1) + coords(1) + images,
    )(turns, points, packs[2], head, *near, *middle)
    tiles = near + middle + stay(far)

    parts = lax.all_to_all(part0.reshape(16, 4, 16, 128), "grid", 0, 0)
    image0, copies = call(
        gather_kernel, "gather", [VM], [array(4, 16, 128), array(16, 4, 16, 128, dtype=BF16)]
    )(parts)
    rounded = lax.all_to_all(copies, "grid", 0, 0)

    packed, part1, sums, along = call(
        functools.partial(again_kernel, scale),
        "again",
        [VM] * 26,
        [array(64, 1024, dtype=BF16), image_type, array(8, EDGE), array(8, 128)],
        weights(1) + weights(2) + weights(1) + images + [pltpu.VMEM((32, 1024), F32)],
        work=8 << 30,
    )(rounded, grad0, *tiles)

    near_hop = ahead(packed, 1)
    hops = [packed, near_hop, ahead(near_hop, 1), ahead(packed, 3)]
    parts = lax.all_to_all(part1.reshape(16, 4, 16, 128), "grid", 0, 0)
    sent = call(
        spread_kernel,
        "spread",
        [SM, SM] + [VM] * 8,
        array(16, 48, 128, dtype=BF16),
        [pltpu.VMEM((4, 16, 128), F32)] * 2,
    )(mic, grid_at, parts, image0, sums, along, *packs)
    recv = lax.all_to_all(sent, ("mic", "bin"), 0, 0)
    sent, alongs = call(relay_kernel, "relay", [SM, VM], [array(16, 144, 128, dtype=BF16), array(8, 128)])(bin_at, recv)
    recv = lax.all_to_all(sent, "grid", 0, 0)
    out_type = array(4, 2, 16, 1024)
    return call(
        last_kernel,
        "last",
        [SM] + [VM] * 7,
        [out_type, out_type],
    )(mic, recv, alongs, press, *hops)


def solution(mesh):
    placed = (P(None, "grid"), P(None, "mic"), P("bin"), P("bin", None, None, "mic"))
    return jax.shard_map(
        body,
        mesh=mesh,
        in_specs=placed,
        out_specs=(P("bin", None, None, "grid"), P("bin", None, None, "mic")),
        check_vma=False,
    )
```

```python
import functools
import math

import jax
import jax.numpy as jnp
from jax import lax
from jax.experimental import pallas as pl
from jax.experimental.pallas import tpu as pltpu
from jax.sharding import PartitionSpec as P

F32, BF16 = jnp.float32, jnp.bfloat16
QUARTER = (2.641753911972046, -1.0863767862319946, 0.13400563597679138, -0.0077399080619215965)
SQUARE = 2.0 * math.sqrt(2.0)
ROOT = math.sqrt(2.0)
ROWS, LANES, EDGE = 16, 256, 256
VM = pl.BlockSpec(memory_space=pltpu.VMEM)
SM = pl.BlockSpec(memory_space=pltpu.SMEM)
ANY = pl.BlockSpec(memory_space=pl.ANY)
HBM = pl.BlockSpec(memory_space=pltpu.HBM)


def steering(gx, gy, gz, mx, my, mz, turns):
    dx, dy, dz = gx - mx, gy - my, gz - mz
    square = dx * dx + dy * dy + dz * dz
    inverse = lax.rsqrt(square)
    cycles = (square * inverse) * turns
    part = cycles - jnp.round(cycles)
    t = part * part
    s = QUARTER[3]
    for k in (2, 1, 0):
        s = s * t + QUARTER[k]
    s = s * part
    q = s * s
    w = SQUARE - q
    half_sin = s * (w * lax.rsqrt(w))
    half_cos = ROOT - q
    scaled = half_sin * inverse
    return (inverse - scaled * half_sin).astype(BF16), (scaled * half_cos).astype(BF16)


def dot_nt(a, b):
    return lax.dot_general(a, b, (((1,), (1,)), ((), ())), preferred_element_type=F32)


def dot_nn(a, b):
    return lax.dot_general(a, b, (((1,), (0,)), ((), ())), preferred_element_type=F32)


def multiple(x, m):
    return x if isinstance(x, int) else pl.multiple_of(x, m)


def span(index):
    return pl.ds(multiple(index * EDGE, EDGE), EDGE)


def lane_sums(x):
    return jnp.sum(x, axis=0, keepdims=True)


def swapped(v):
    return jnp.concatenate([v[16:32], -v[0:16]], axis=0)


class Tiles:
    def __init__(self, refs):
        self.refs = refs

    def get(self, step_odd, chunk_odd):
        at = (step_odd * 2 + chunk_odd) * 2
        return self.refs[at], self.refs[at + 1]

    def build(self, grid_ref, mics, turns, half, odd, pair, chunk_odd):
        c_ref, s_ref = self.get(odd, chunk_odd)
        for block in range(EDGE // ROWS):
            rows = pl.ds(multiple((half * 2 + odd) * EDGE + block * ROWS, ROWS), ROWS)
            g = [jnp.broadcast_to(grid_ref[rows, d : d + 1], (ROWS, LANES)) for d in range(3)]
            c, s = steering(*g, *mics, turns)
            at = (pl.ds(multiple(half * EDGE + block * ROWS, ROWS), ROWS), span(pair))
            c_ref[at] = c
            s_ref[at] = s

    def adjoint(self, weights, half, odd, pair, chunk_odd):
        c_ref, s_ref = self.get(odd, chunk_odd)
        wc, ws = weights[0], weights[1]
        at = (span(half), span(pair))
        cols = span(pair)
        return dot_nt(wc[chunk_odd, :, cols], c_ref[at]) + dot_nt(ws[chunk_odd, :, cols], s_ref[at])

    def forward(self, image, v, v2, half, odd, pair, chunk_odd):
        c_ref, s_ref = self.get(odd, chunk_odd)
        at = (span(half), span(pair))
        image[chunk_odd, :, span(pair)] += dot_nn(v, c_ref[at]) + dot_nn(v2, s_ref[at])


def three(x):
    high = x.astype(BF16).astype(F32)
    left = x - high
    middle = left.astype(BF16).astype(F32)
    return high, middle, (left - middle).astype(BF16).astype(F32)


def prepare_kernel(mic_ref, bin_ref, grid_ref, wave_hbm, press_hbm, coords_hbm, points_hbm, g_ref, turns_ref, p0, p1, p2, p3, press, *scratch):
    wave_ref, coords, pad, sems = scratch
    copies = [
        pltpu.make_async_copy(press_hbm, press, sems.at[0]),
        pltpu.make_async_copy(coords_hbm, coords, sems.at[1]),
        pltpu.make_async_copy(points_hbm, pad.at[0:3], sems.at[2]),
        pltpu.make_async_copy(wave_hbm, wave_ref, sems.at[3]),
    ]
    for copy in copies:
        copy.start()
    for copy in copies:
        copy.wait()
    turns_ref[...] = jnp.full((8, 128), wave_ref[mic_ref[0]] * (0.5 / math.pi), F32)
    high, middle, low = [part.astype(BF16) for part in three(coords[...])]
    for s, out in enumerate((p0, p1, p2, p3)):
        out[0:32] = press[lax.rem(mic_ref[0] + 4 - s, 4)].astype(BF16)
        out[32:35], out[35:38], out[38:41] = high, middle, low
        out[41:48] = jnp.zeros((7, 1024), BF16)
    pad[3:8] = jnp.zeros((5, 1024), F32)
    for r in range(8):
        g_ref[r * 128 : r * 128 + 128, :] = pad[:, r * 128 : r * 128 + 128].T


def whole_coords(pack):
    parts = pack[32:48].astype(F32)
    return (parts[0:3] + parts[3:6]) + parts[6:9]


def set_weights(wc, ws, chunk, real, imag, scale):
    odd, cols = chunk % 2, slice((chunk // 2) * EDGE, (chunk // 2) * EDGE + EDGE)
    real, imag = real * scale, imag * scale
    wc[odd, 0:16, cols] = real
    wc[odd, 16:32, cols] = imag
    ws[odd, 0:16, cols] = -imag
    ws[odd, 16:32, cols] = real


def head_kernel(scale, count, turns_ref, grid_ref, *refs):
    packs, refs = refs[:count], refs[count:]
    if count > 1:
        before, refs = refs[0], refs[1:]
    tiles, (grad_ref, wc, ws, coords) = Tiles(refs[:8]), refs[8:]
    turns = turns_ref[0:1, 0:1]
    for s, pack in enumerate(packs):
        for chunk in range(4):
            w = pack[0:32, chunk * EDGE : chunk * EDGE + EDGE]
            set_weights(wc, ws, s * 4 + chunk, w[0:16], w[16:32], scale)
        coords[0:3, s * 1024 : s * 1024 + 1024] = whole_coords(pack)

    def mics(chunk):
        return [coords[d : d + 1, chunk * EDGE : chunk * EDGE + EDGE] for d in range(3)]

    def half_step(half, carry):
        late = done = None
        for odd in range(2):
            total = jnp.zeros((32, EDGE), F32) if count == 1 else before[:, span(half * 2 + odd)]
            for pair in range(2 * count):
                for chunk_odd in range(2):
                    if late is not None:
                        value = tiles.adjoint((wc, ws), half, *late)
                        if late[0] == odd:
                            total += value
                        else:
                            grad_ref[:, span(half * 2 + late[0])] = done + value
                    tiles.build(grid_ref, mics(pair * 2 + chunk_odd), turns, half, odd, pair, chunk_odd)
                    late = (odd, pair, chunk_odd)
            done = total
        grad_ref[:, span(half * 2 + 1)] = done + tiles.adjoint((wc, ws), half, *late)
        return carry

    lax.fori_loop(0, 2, half_step, 0)


def store_image(out_ref, image, blocks):
    for odd in range(2):
        for pair in range(image.shape[2] // EDGE):
            for piece in range(2):
                tile = (pair * 2 + odd) * 2 + piece
                s, c = blocks[tile // 8], tile % 8
                lo = pair * EDGE + piece * 128
                for h in range(2):
                    out_ref[c, h, s] = image[odd, h * 16 : h * 16 + 16, lo : lo + 128].astype(BF16)


BLOCKS = ((0,), (1, 3), (2,))


def rest_kernel(scale, turns_ref, grid_ref, pack, before, *refs):
    near, middle, tiles = Tiles(refs[:8]), Tiles(refs[8:16]), Tiles(refs[16:24])
    grad_ref, image_ref, wc, ws, coords = refs[24:29]
    images = refs[29:]
    turns = turns_ref[0:1, 0:1]
    for chunk in range(4):
        w = pack[0:32, chunk * EDGE : chunk * EDGE + EDGE]
        set_weights(wc, ws, chunk, w[0:16], w[16:32], scale)
    coords[0:3] = whole_coords(pack)
    for image in images:
        image[...] = jnp.zeros_like(image)
    tasks = []
    for group, image, blocks in zip((near, middle, tiles), images, BLOCKS):
        tasks += [(group, image, pair, odd) for pair in range(2 * len(blocks)) for odd in range(2)]

    def forward(some, v, half, odd):
        for group, image, pair, chunk_odd in some:
            group.forward(image, *v, half, odd, pair, chunk_odd)

    v = last = None
    for half, odd in ((0, 0), (0, 1), (1, 0), (1, 1)):
        total = before[:, span(half * 2 + odd)]
        for n in range(4):
            if n:
                total += tiles.adjoint((wc, ws), half, odd, *divmod(n - 1, 2))
            if last is not None:
                forward(tasks[4 * n : 4 * n + 4], v, *last)
            cols = slice(n * EDGE, n * EDGE + EDGE)
            tiles.build(grid_ref, [coords[d : d + 1, cols] for d in range(3)], turns, half, odd, *divmod(n, 2))
        total += tiles.adjoint((wc, ws), half, odd, 1, 1)
        grad_ref[:, span(half * 2 + odd)] = total
        v = total.astype(BF16) * scale
        v, last = (v, swapped(v)), (half, odd)
    forward(tasks, v, *last)
    for image, blocks in zip(images, BLOCKS):
        store_image(image_ref, image, blocks)


def again_kernel(scale, q_ref, grad0_ref, *refs):
    groups = Tiles(refs[:8]), Tiles(refs[8:16]), Tiles(refs[16:24])
    packed_ref, image_ref, sums_ref, along_ref, *refs = refs[24:]
    weights, images, grad_ref = (refs[0:2], refs[2:4], refs[4:6]), refs[6:9], refs[9]
    for pair, blocks in zip(weights, BLOCKS):
        for at, block in enumerate(blocks):
            for chunk in range(4):
                real = jnp.concatenate([q_ref[4 * chunk + 2 * p, block] for p in range(2)], axis=1)
                imag = jnp.concatenate([q_ref[4 * chunk + 2 * p + 1, block] for p in range(2)], axis=1)
                set_weights(*pair, at * 4 + chunk, real, imag, scale)
    for image in images:
        image[...] = jnp.zeros_like(image)
    sums_ref[...] = jnp.zeros_like(sums_ref)

    def forward(v, half, odd):
        for o in range(2):
            for image, group in zip(images, groups):
                c_ref, s_ref = group.get(odd, o)
                image[o] += dot_nn(v[0], c_ref[span(half), :]) + dot_nn(v[1], s_ref[span(half), :])

    def adjoint(half, odd):
        total = None
        for o in range(2):
            for (w_c, w_s), group in zip(weights, groups):
                c_ref, s_ref = group.get(odd, o)
                value = dot_nt(c_ref[span(half), :], w_c[o]) + dot_nt(s_ref[span(half), :], w_s[o])
                total = value if total is None else total + value
        return total.T

    def finish(half, odd, total):
        cols = span(half * 2 + odd)
        g0 = grad0_ref[:, cols]
        grad_ref[:, cols] = total
        sums_ref[0:1] += lane_sums(g0 * g0)
        sums_ref[1:2] += lane_sums(g0 * total)
        sums_ref[2:3] += lane_sums(total * total)
        v = total.astype(BF16) * scale
        return v, swapped(v)

    v = finish(0, 0, adjoint(0, 0))
    for half, odd, before in ((0, 1, (0, 0)), (1, 0, (0, 1)), (1, 1, (1, 0))):
        total = adjoint(half, odd)
        forward(v, *before)
        v = finish(half, odd, total)
    forward(v, 1, 1)
    for image, blocks in zip(images, BLOCKS):
        store_image(image_ref, image, blocks)
    gg = jnp.sum(sums_ref[0:1], axis=1, keepdims=True)
    gh = jnp.sum(sums_ref[1:2], axis=1, keepdims=True)
    along = coefficient(gg, gh)
    along_ref[...] = jnp.broadcast_to(along, (8, 128))
    packed_ref[0:32] = grad0_ref[...].astype(BF16)
    packed_ref[32:64] = (grad_ref[...] - along * grad0_ref[...]).astype(BF16)


def coefficient(aa, ab):
    value = jnp.where(aa > 0.0, ab / jnp.where(aa > 0.0, aa, 1.0), 0.0)
    return value.astype(BF16).astype(F32)


def total_of(parts_ref):
    total = parts_ref[0].astype(F32)
    for j in range(1, 16):
        total += parts_ref[j].astype(F32)
    return total


def gather_kernel(parts_ref, shard_ref, copies_ref):
    total = total_of(parts_ref)
    shard_ref[...] = total
    low = total.astype(BF16)
    for j in range(16):
        copies_ref[j] = low


def pack_sums(sums, rest):
    high, middle, low = three(sums[:, 0:64] + sums[:, 64:128])
    left = jnp.concatenate([high, low], axis=0)
    right = jnp.concatenate([middle, jnp.zeros_like(low)], axis=0)
    return jnp.concatenate([jnp.concatenate([left, right], axis=1), rest], axis=0).astype(BF16)


def unpack_sums(tile):
    tile = tile.astype(F32)
    return tile[0:6] + jnp.concatenate([tile[6:12, 0:64], jnp.zeros((6, 64), F32)], axis=1), tile[12:16]


def sums_of(recv_ref, at):
    total = recv_ref[0, at : at + 16].astype(F32)
    for j in range(1, 16):
        total += recv_ref[j, at : at + 16].astype(F32)
    return unpack_sums(total)[0]


def spread_kernel(mic_ref, grid_ref, parts_ref, q_ref, sums_ref, along_ref, p0, p1, p2, p3, out_ref, off_press, off_image):
    total = total_of(parts_ref)
    q = q_ref[...]
    rows = pl.ds(pl.multiple_of(lax.rem(grid_ref[0], 2) * 16, 16), 16)
    cols = pl.ds(pl.multiple_of(lax.div(grid_ref[0], 2) * 128, 128), 128)
    press = jnp.stack([pack[rows, cols] for pack in (p0, p1, p2, p3)]).astype(F32)

    def flat(x):
        return lane_sums(x.reshape(64, 128))

    def part_along(aa, ab):
        return coefficient(jnp.sum(aa, axis=1, keepdims=True), jnp.sum(ab, axis=1, keepdims=True))

    near = sums_ref[0:3, 0:128] + sums_ref[0:3, 128:256]
    qq, qp = flat(q * q), flat(q * total)
    sums = jnp.concatenate([near, qq, qp, flat(total * total)], axis=0)
    on_press = part_along(flat(press * press), flat(press * q))
    on_image = part_along(qq, qp)
    off_press[...] = q - on_press * press
    off_image[...] = total - on_image * q
    both = jnp.concatenate([jnp.broadcast_to(on_image, (1, 64)), jnp.broadcast_to(on_press, (1, 64))], axis=1)
    tile = pack_sums(sums, jnp.concatenate([both, along_ref[0:1], jnp.zeros((2, 128), F32)], axis=0))
    for t in range(4):
        s = lax.rem(t + 4 - mic_ref[0], 4)
        first, second = off_press[s].astype(BF16), off_image[s].astype(BF16)
        for k in range(4):
            out_ref[t * 4 + k, 0:16] = first
            out_ref[t * 4 + k, 16:32] = second
            out_ref[t * 4 + k, 32:48] = tile


def relay_kernel(bin_ref, recv_ref, out_ref, along_ref):
    sums = sums_of(recv_ref, 32)
    rest = []
    for m in range(4):
        slot = m * 4 + bin_ref[0]
        piece = recv_ref[slot, 0:32]
        for j in range(16):
            out_ref[j, m * 32 : m * 32 + 32] = piece
        values = recv_ref[slot, 32:48].astype(F32)
        rest.append(values[12:13])
        along_ref[m : m + 1] = values[13:14]
    along_ref[4:8] = jnp.zeros((4, 128), F32)
    tile = pack_sums(sums, jnp.concatenate(rest, axis=0))
    for j in range(16):
        out_ref[j, 128:144] = tile


def last_kernel(mic_ref, recv_ref, along_ref, press_ref, *refs):
    packs, (x_ref, r_ref) = refs[:4], refs[4:]
    total = jnp.sum(sums_of(recv_ref, 128), axis=1, keepdims=True)
    gg, gh, hh, qq, qp, pp = [total[i : i + 1] for i in range(6)]
    step0 = gg / qq
    norm1 = gg - 2.0 * step0 * gh + step0 * step0 * hh
    ratio = norm1 / gg
    image1 = (1.0 + ratio) * (1.0 + ratio) * qq - 2.0 * (1.0 + ratio) * step0 * qp + step0 * step0 * pp
    step1 = norm1 / image1
    lead = jnp.broadcast_to(step0 + step1 * (1.0 + ratio), (16, 128))
    tail = jnp.broadcast_to(step0 * step1, (16, 128))
    for s, pack in enumerate(packs):
        bin_at = lax.rem(mic_ref[0] + s, 4)
        first = lead - tail * along_ref[pl.ds(bin_at, 1)]
        for h in range(2):
            for c in range(8):
                cols = slice(c * 128, c * 128 + 128)
                g = pack[h * 16 : h * 16 + 16, cols].astype(F32)
                y = pack[32 + h * 16 : 48 + h * 16, cols].astype(F32)
                x_ref[bin_at, h, :, cols] = first * g - tail * y
    for h in range(2):
        for c in range(8):
            j, cols = 2 * c + h, slice(c * 128, c * 128 + 128)
            rest = unpack_sums(recv_ref[j, 128:144])[1]
            for m in range(4):
                press = press_ref[m, h * 16 : h * 16 + 16, cols]
                q = recv_ref[j, m * 32 : m * 32 + 16].astype(F32)
                q += rest[m : m + 1, 64:65] * press.astype(BF16).astype(F32)
                off = recv_ref[j, m * 32 + 16 : m * 32 + 32].astype(F32)
                r_ref[m, h, :, cols] = press - (lead - tail * rest[m : m + 1, 0:1]) * q + tail * off


def call(kernel, name, in_specs, out_shape, scratch=(), limit=4, work=0):
    return pl.pallas_call(
        kernel,
        in_specs=in_specs,
        out_specs=jax.tree.map(lambda _: VM, out_shape),
        out_shape=out_shape,
        scratch_shapes=list(scratch),
        compiler_params=pltpu.CompilerParams(vmem_limit_bytes=limit << 20),
        cost_estimate=pl.CostEstimate(flops=work, bytes_accessed=0, transcendentals=0) if work else None,
        name=name,
    )


def array(*shape, dtype=F32):
    return jax.ShapeDtypeStruct(shape, dtype)


def ahead(x, shift):
    return lax.ppermute(x, "mic", [((t + shift) % 4, t) for t in range(4)])


def body(grid_points, mic_coords, wavenumbers, pressures):
    scale = 1.0 / math.sqrt(grid_points.shape[1] * lax.axis_size("grid"))
    mic, bin_at, grid_at = [jnp.reshape(lax.axis_index(name), (1,)).astype(jnp.int32) for name in ("mic", "bin", "grid")]
    flat = pressures.reshape(4, 32, 1024)

    points, turns, *packs, press = call(
        prepare_kernel,
        "prepare",
        [SM, SM, SM, HBM, HBM, HBM, HBM],
        [pltpu.VMEM((1024, 8), F32), pltpu.VMEM((8, 128), F32)] + [pltpu.VMEM((48, 1024), BF16)] * 4
        + [pltpu.VMEM((4, 32, 1024), F32)],
        [
            pltpu.SMEM((4,), F32),
            pltpu.VMEM((3, 1024), F32),
            pltpu.VMEM((8, 1024), F32),
            pltpu.SemaphoreType.DMA((4,)),
        ],
        limit=60,
    )(mic, bin_at, grid_at, wavenumbers, flat, mic_coords, grid_points)
    packs[1:] = [ahead(pack, s) for s, pack in zip((1, 2, 3), packs[1:])]

    def held(width):
        return [pltpu.VMEM((512, width), BF16)] * 8

    def weights(count):
        return [pltpu.VMEM((2, 32, 512 * count), BF16)] * 2

    def coords(count):
        return [pltpu.VMEM((8, 1024 * count), F32)]

    images = [pltpu.VMEM((2, 32, 512 * len(blocks)), F32) for blocks in BLOCKS]
    image_type = array(8, 2, 4, 16, 128, dtype=BF16)

    def stay(tiles):
        return [pltpu.with_memory_space_constraint(t, pltpu.VMEM) for t in tiles]

    *near, head = call(
        functools.partial(head_kernel, scale, 1),
        "own",
        [VM] * 3,
        held(512) + [array(32, 1024)],
        weights(1) + coords(1),
    )(turns, points, packs[0])
    near = stay(near)
    *middle, head = call(
        functools.partial(head_kernel, scale, 2),
        "middle",
        [VM] * 5,
        held(1024) + [array(32, 1024)],
        weights(2) + coords(2),
    )(turns, points, packs[1], packs[3], head)
    middle = stay(middle)
    *far, grad0, part0 = call(
        functools.partial(rest_kernel, scale),
        "rest",
        [VM] * 20,
        held(512) + [array(32, 1024), image_type],
        weights(1) + coords(1) + images,
    )(turns, points, packs[2], head, *near, *middle)
    tiles = near + middle + stay(far)

    parts = lax.all_to_all(part0.reshape(16, 4, 16, 128), "grid", 0, 0)
    image0, copies = call(
        gather_kernel, "gather", [VM], [array(4, 16, 128), array(16, 4, 16, 128, dtype=BF16)]
    )(parts)
    rounded = lax.all_to_all(copies, "grid", 0, 0)

    packed, part1, sums, along = call(
        functools.partial(again_kernel, scale),
        "again",
        [VM] * 26,
        [array(64, 1024, dtype=BF16), image_type, array(8, EDGE), array(8, 128)],
        weights(1) + weights(2) + weights(1) + images + [pltpu.VMEM((32, 1024), F32)],
        work=8 << 30,
    )(rounded, grad0, *tiles)

    near_hop = ahead(packed, 1)
    hops = [packed, near_hop, ahead(near_hop, 1), ahead(packed, 3)]
    parts = lax.all_to_all(part1.reshape(16, 4, 16, 128), "grid", 0, 0)
    sent = call(
        spread_kernel,
        "spread",
        [SM, SM] + [VM] * 8,
        array(16, 48, 128, dtype=BF16),
        [pltpu.VMEM((4, 16, 128), F32)] * 2,
    )(mic, grid_at, parts, image0, sums, along, *packs)
    recv = lax.all_to_all(sent, ("mic", "bin"), 0, 0)
    sent, alongs = call(relay_kernel, "relay", [SM, VM], [array(16, 144, 128, dtype=BF16), array(8, 128)])(bin_at, recv)
    recv = lax.all_to_all(sent, "grid", 0, 0)
    out_type = array(4, 2, 16, 1024)
    return call(
        last_kernel,
        "last",
        [SM] + [VM] * 7,
        [out_type, out_type],
    )(mic, recv, alongs, press, *hops)


def solution(mesh):
    placed = (P(None, "grid"), P(None, "mic"), P("bin"), P("bin", None, None, "mic"))
    return jax.shard_map(
        body,
        mesh=mesh,
        in_specs=placed,
        out_specs=(P("bin", None, None, "grid"), P("bin", None, None, "mic")),
        check_vma=False,
    )
```
